512 devices in a mesh: blk: 64 (over x, y, core), body: 8 (over z).
Axes of the slice: x: 4, y: 8, z: 8, core: 2. Of those that a mesh axis runs over, the one named last changes fastest.
Arguments:
- positions: float32 [3, 1048576], P(None, ('blk', 'body')), may hold values from -2.5 to 2.5
- direction: float32 [3, 1048576], P(None, ('blk', 'body')), may hold values from -6 to 6
- pair_local: int32 [32768], P(('blk', 'body')), may hold values from 0 to 15
- pair_peer: int32 [32768], P(('blk', 'body')), may hold values from 0 to 63, as said below
- pair_shift: int32 [32768], P(('blk', 'body')), may hold values from 1 to 15
- pair_count: int32 [512], P(('blk', 'body')), may hold values from 32 to 64, as said below
- face_index: int32 [2048], P(('blk', 'body')), may hold values from 0 to 15
- cross_local: int32 [4096], P(('blk', 'body')), may hold values from 0 to 15
- cross_face: int32 [4096], P(('blk', 'body')), may hold values from 0 to 3
Outputs:
- gradient: float32 [3, 1048576], P(None, ('blk', 'body'))
- hess_dir: float32 [3, 1048576], P(None, ('blk', 'body'))
The draws below stay inside these ranges and needn't reach their ends.
Inputs may be any that keep to these rules, and one draw needn't show every extreme that they name: `pair_peer`: among the 64 slots of one device, used or not, at most 2 name the same peer; in every draw some device has 2 slots naming one peer. `pair_count`: some device uses all 64 slots.
All inputs are finite; a program needn't handle non-finite values.
Results may differ from the reference program's by a relative error of at most 0.0003.
Values sent between devices are 32-bit elements; how exact they have to be, the bound alone decides.
No kernel may reach another device: no remote copies, remote signals or barrier semaphores. Data moves between devices by JAX's collectives and lax.ppermute only.
A program may use at most 64 MiB of HBM per device.

```python
import jax
import jax.numpy as jnp
from jax import lax

BLOCK = 128
NB_DEV = 16
PAIRS_DEV = 64
FACES_DEV = 4
XPAIRS_DEV = 8
NPEER = 64
NBODY = 8
NDEV = 512
CAP = 2
VERTS = 1048576
PAIRS = 32768
FACES = 2048
XPAIRS = 4096


def draw_pair_peer(key, part):
    slot_total = NPEER * CAP

    def one_device(device_key):
        order = jax.random.permutation(device_key, slot_total)
        chosen_peer = order[0] // CAP
        special = (order // CAP == chosen_peer).astype(jnp.int32)
        ranked = jnp.argsort(1 - special, stable=True)
        picked = order[ranked][:PAIRS_DEV]
        return (picked // CAP).astype(jnp.int32)
    device_keys = jax.random.split(key, NDEV)
    return jax.vmap(one_device)(device_keys).reshape(NDEV * PAIRS_DEV).astype(jnp.int32)


def draw_pair_count(key, part):
    key_counts, key_top = jax.random.split(jax.random.fold_in(key, 7))
    counts = jax.random.randint(key_counts, (NDEV,), PAIRS_DEV // 2, 3 * PAIRS_DEV // 4 + 1)
    busiest = jax.random.randint(key_top, (), 0, NDEV)
    return jnp.where(jnp.arange(NDEV) == busiest, PAIRS_DEV, counts).astype(jnp.int32)


def place_ends(array, stream_key, least, largest):
    index_at = [jax.random.randint(jax.random.fold_in(stream_key, axis), (), 0, length) for axis, length in enumerate(array.shape)]
    main_axis = array.shape.index(max(array.shape))
    next_to = index_at[:main_axis] + [(index_at[main_axis] + 1) % array.shape[main_axis]] + index_at[main_axis + 1:]
    return array.at[tuple(index_at)].set(least).at[tuple(next_to)].set(largest)


def block_levels(own_key, extent, cuts, least, largest):
    def one(dim, blocks):
        steps = jax.random.uniform(jax.random.fold_in(jax.random.fold_in(own_key, 6), dim), (blocks,), jnp.float32, least / len(cuts), largest / len(cuts))
        return jnp.repeat(jnp.exp(steps), extent[dim] // blocks).reshape((-1,) + (1,) * (len(extent) - dim - 1))

    loudness = one(*cuts[0])
    for cut in cuts[1:]:
        loudness = loudness * one(*cut)
    return loudness


def normal_values(stream_key, dims, width, bound, pieces=(), kind=jnp.bfloat16):
    array = jax.random.normal(stream_key, dims, jnp.float32) * width
    if len(pieces) > 0:
        array = block_levels(stream_key, dims, pieces, -0.22, 0.18) * array
    return jnp.clip(array, min=-bound, max=bound).astype(kind)


def setup_inputs(seed: int = 0) -> dict:
    seeds = jax.random.split(jax.random.key(seed), 10)
    return {
        "positions": normal_values(seeds[0], (3, VERTS), 0.35, 2.5, ((1, 512),), jnp.float32),
        "direction": normal_values(seeds[1], (3, VERTS), 1.0, 6.0, ((1, 512),), jnp.float32),
        "pair_local": place_ends(jax.random.randint(seeds[2], (PAIRS,), 0, NB_DEV), jax.random.fold_in(seeds[2], 1), 0, NB_DEV - 1).astype(jnp.int32),
        "pair_peer": draw_pair_peer(jax.random.fold_in(seeds[9], 71), 0),
        "pair_shift": place_ends(jax.random.randint(seeds[4], (PAIRS,), 1, NB_DEV), jax.random.fold_in(seeds[4], 1), 1, NB_DEV - 1).astype(jnp.int32),
        "pair_count": draw_pair_count(jax.random.fold_in(seeds[9], 71), 0),
        "face_index": place_ends(jax.random.randint(seeds[6], (FACES,), 0, NB_DEV), jax.random.fold_in(seeds[6], 1), 0, NB_DEV - 1).astype(jnp.int32),
        "cross_local": place_ends(jax.random.randint(seeds[7], (XPAIRS,), 0, NB_DEV), jax.random.fold_in(seeds[7], 1), 0, NB_DEV - 1).astype(jnp.int32),
        "cross_face": place_ends(jax.random.randint(seeds[8], (XPAIRS,), 0, FACES_DEV), jax.random.fold_in(seeds[8], 1), 0, FACES_DEV - 1).astype(jnp.int32),
    }


XI = 0.1
SHAT = 1.0
KAPPA = 0.02


def pair_terms(near, far):
    near_pos = near[:, :3]
    near_dir = near[:, 3:]
    far_pos = far[:, :3]
    far_dir = far[:, 3:]
    offset = near_pos[:, :, :, None] - far_pos[:, :, None, :]
    motion = near_dir[:, :, :, None] - far_dir[:, :, None, :]
    squared = jnp.sum(offset * offset, axis=1) + XI
    excess = squared - SHAT
    log_ratio = jnp.log(squared / SHAT)
    active = squared < SHAT
    first_slope = jnp.where(active, -2.0 * excess * log_ratio - excess * excess / squared, 0.0)
    second = jnp.where(active, -2.0 * log_ratio - 4.0 * excess / squared + excess * excess / (squared * squared), 0.0)
    grad_coef = 2.0 * KAPPA * first_slope
    curv_coef = 4.0 * KAPPA * second * jnp.sum(offset * motion, axis=1)
    forces = grad_coef[:, None] * offset
    curves = curv_coef[:, None] * offset + grad_coef[:, None] * motion
    near_terms = jnp.concatenate([jnp.sum(forces, axis=3), jnp.sum(curves, axis=3)], axis=1)
    far_terms = -jnp.concatenate([jnp.sum(forces, axis=2), jnp.sum(curves, axis=2)], axis=1)
    return near_terms, far_terms


def reference(positions, direction, pair_local, pair_peer, pair_shift, pair_count, face_index, cross_local, cross_face):
    blocks_all = jnp.concatenate([positions, direction], axis=0).reshape(6, NDEV * NB_DEV, BLOCK).transpose(1, 0, 2)

    def advance(totals, device):
        body_slot = device % NBODY
        near_local = lax.dynamic_slice_in_dim(pair_local, device * PAIRS_DEV, PAIRS_DEV)
        peer_ids = lax.dynamic_slice_in_dim(pair_peer, device * PAIRS_DEV, PAIRS_DEV)
        shifts = lax.dynamic_slice_in_dim(pair_shift, device * PAIRS_DEV, PAIRS_DEV)
        near_id = device * NB_DEV + near_local
        far_id = (peer_ids * NBODY + body_slot) * NB_DEV + (near_local + shifts) % NB_DEV
        in_use = (jnp.arange(PAIRS_DEV, dtype=jnp.int32) < pair_count[device]).astype(blocks_all.dtype)[:, None, None]
        near_terms, far_terms = pair_terms(blocks_all[near_id], blocks_all[far_id])
        left_dev = jnp.maximum(device - 1, 0).astype(jnp.int32)
        face_rows = lax.dynamic_slice_in_dim(face_index, left_dev * FACES_DEV, FACES_DEV)
        cross_here = lax.dynamic_slice_in_dim(cross_local, device * XPAIRS_DEV, XPAIRS_DEV)
        cross_pick = lax.dynamic_slice_in_dim(cross_face, device * XPAIRS_DEV, XPAIRS_DEV)
        cross_near_id = device * NB_DEV + cross_here
        cross_far_id = left_dev * NB_DEV + face_rows[cross_pick]
        has_left = (body_slot > 0).astype(blocks_all.dtype)
        cross_near, cross_far = pair_terms(blocks_all[cross_near_id], blocks_all[cross_far_id])
        totals = totals.at[near_id].add(near_terms * in_use)
        totals = totals.at[far_id].add(far_terms * in_use)
        totals = totals.at[cross_near_id].add(cross_near * has_left)
        totals = totals.at[cross_far_id].add(cross_far * has_left)
        return totals, None

    totals, _ = lax.scan(advance, jnp.zeros_like(blocks_all), jnp.arange(NDEV, dtype=jnp.int32))
    merged = totals.transpose(1, 0, 2).reshape(6, NDEV * NB_DEV * BLOCK)
    return merged[:3], merged[3:]
```

```python
import jax
import jax.numpy as jnp
from jax import lax
from jax.experimental import pallas as pl
from jax.experimental.pallas import tpu as pltpu
from jax.sharding import PartitionSpec as P

XI = 0.1
SCALE = 0.04
LANES = 128
MSG = 13
RET = 12
F32 = jnp.float32
BF16 = jnp.bfloat16
NN = (((1,), (0,)), ((), ()))
NT = (((1,), (1,)), ((), ()))


def from_behind(value, axis, steps):
    count = lax.axis_size(axis)
    first, last = (max(0, -steps), min(count, count - steps))
    return lax.ppermute(value, axis, [(source, source + steps) for source in range(first, last)])


def block_rows(pos_ref, dir_ref, block):
    cols = pl.ds(pl.multiple_of(block * LANES, LANES), LANES)
    return pos_ref[:, cols], dir_ref[:, cols]


def pack_kernel(
    local_ref, peer_ref, shift_ref, count_ref, face_ref, pos_ref, dir_ref,
    send_ref, faces_ref, slot_ref, used_ref,
):
    peers = used_ref.shape[0]
    num_blocks = pos_ref.shape[1] // LANES
    lane = lax.broadcasted_iota(jnp.int32, (1, LANES), 1)
    unused = jnp.full((1, LANES), -1.0, F32)
    for face in range(face_ref.shape[0]):
        near_pos, near_dir = block_rows(pos_ref, dir_ref, face_ref[face])
        faces_ref[face * 6 : face * 6 + 3, :] = near_pos
        faces_ref[face * 6 + 3 : face * 6 + 6, :] = near_dir
    for peer in range(peers):
        used_ref[peer] = 0
        row = peer * MSG + RET
        send_ref[row : row + 1, :] = unused

    def one(pair, carry):
        near = local_ref[pair]
        peer = peer_ref[pair]
        far = lax.rem(near + shift_ref[pair], num_blocks)
        rank = used_ref[peer]
        used_ref[peer] = rank + 1
        slot_ref[pair] = peer * RET + rank * 6
        near_pos, near_dir = block_rows(pos_ref, dir_ref, near)
        base = peer * MSG
        send_ref[pl.ds(base + rank * 6, 3), :] = near_pos
        send_ref[pl.ds(base + rank * 6 + 3, 3), :] = near_dir
        row = pl.ds(base + RET, 1)
        send_ref[row, :] = jnp.where(lane == rank, far.astype(F32), send_ref[row, :])
        return carry

    lax.fori_loop(0, count_ref[0], one, 0)


def pieces(value):
    high = value.astype(BF16)
    rest = value - high.astype(F32)
    mid = rest.astype(BF16)
    low = (rest - mid.astype(F32)).astype(BF16)
    return high, mid, low


def stacked(rows):
    high, mid, low = pieces(rows)
    tall = jnp.concatenate([high, mid, low, jnp.zeros_like(low)], axis=0)
    return jnp.concatenate([tall, tall], axis=1)


def local_setup(pos_ref, dir_ref, rows_ref, cols_ref, left_ref, center_ref):
    row = lax.broadcasted_iota(jnp.int32, (8, LANES), 0)
    for block in range(pos_ref.shape[1] // LANES):
        span = slice(block * LANES, (block + 1) * LANES)
        rows = jnp.concatenate(
            [pos_ref[:, span], dir_ref[:, span], jnp.zeros((2, LANES), F32)], axis=0
        )
        center = jnp.mean(rows, axis=1, keepdims=True)
        rows = rows - center
        center_ref[block] = jnp.broadcast_to(center, (8, LANES))
        cols_ref[block] = rows.T
        rows = jnp.where(row == 6, 1.0, rows)
        rows_ref[block] = rows
        left_ref[block] = stacked(rows)


def own_terms(rows, sums):
    row = lax.broadcasted_iota(jnp.int32, (8, LANES), 0)
    by_grad = sums[:, :LANES]
    by_curv = sums[:, LANES:]
    first = rows * by_grad[6:7, :] - by_grad
    second = rows * by_curv[6:7, :] - by_curv
    shifted = pltpu.roll(second, 3, 0)
    return SCALE * (first + jnp.where((row >= 3) & (row < 6), shifted, 0.0))


def fold(product):
    return product[0:8] + product[8:16] + product[16:24]


def one_pair(block, remote, cols_ref, left_ref, center_ref):
    row = lax.broadcasted_iota(jnp.int32, (8, LANES), 0)
    remote = remote - center_ref[block]
    grads, curvs = [], []
    for chunk in range(LANES // 16):
        col = cols_ref[block, chunk * 16 : chunk * 16 + 16, :]
        offset = [col[:, c : c + 1] - remote[c : c + 1, :] for c in range(3)]
        motion = [col[:, c + 3 : c + 4] - remote[c + 3 : c + 4, :] for c in range(3)]
        squared = offset[0] * offset[0] + offset[1] * offset[1] + offset[2] * offset[2] + XI
        along = offset[0] * motion[0] + offset[1] * motion[1] + offset[2] * motion[2]
        squared = jnp.minimum(squared, 1.0)
        log_twice = 2.0 * jnp.log(squared)
        excess = squared - 1.0
        ratio = excess / squared
        grad = -(excess * (log_twice + ratio))
        curv = (ratio * (ratio - 4.0) - log_twice) * (along + along)
        grads.append(grad)
        curvs.append(curv)
    grad = jnp.concatenate(grads, axis=0)
    curv = jnp.concatenate(curvs, axis=0)
    grad_high = grad.astype(BF16)
    grad_low = (grad - grad_high.astype(F32)).astype(BF16)
    curv_high = curv.astype(BF16)
    curv_low = (curv - curv_high.astype(F32)).astype(BF16)
    remote_rows = jnp.where(row == 6, 1.0, remote)
    by_local = jnp.concatenate(
        [
            jnp.concatenate([grad_high, curv_high], axis=1),
            jnp.concatenate([grad_low, curv_low], axis=1),
        ],
        axis=0,
    )
    by_remote = jnp.concatenate(
        [
            jnp.concatenate([grad_high, grad_low], axis=1),
            jnp.concatenate([curv_high, curv_low], axis=1),
        ],
        axis=0,
    )
    for_remote = lax.dot_general(left_ref[block], by_local, NN, preferred_element_type=F32)
    for_local = lax.dot_general(stacked(remote_rows), by_remote, NT, preferred_element_type=F32)
    return own_terms(remote_rows, fold(for_remote)), fold(for_local)


def eight_rows(six):
    return jnp.concatenate([six, jnp.zeros((2, LANES), F32)], axis=0)


def cross_kernel(
    local_ref, face_ref, pos_ref, dir_ref, incoming_ref,
    sums_ref, back_ref,
    rows_ref, cols_ref, left_ref, center_ref,
):
    local_setup(pos_ref, dir_ref, rows_ref, cols_ref, left_ref, center_ref)
    sums_ref[...] = jnp.zeros_like(sums_ref)
    back_ref[...] = jnp.zeros_like(back_ref)

    def one(pair, carry):
        block = local_ref[pair]
        rows = pl.ds(face_ref[pair] * 6, 6)
        remote, local = one_pair(
            block, eight_rows(incoming_ref[rows, :]), cols_ref, left_ref, center_ref
        )
        back_ref[rows, :] += remote[:6]
        sums_ref[block] += local
        return carry

    count = jnp.where(lax.axis_index("body") > 0, local_ref.shape[0], 0)
    lax.fori_loop(0, count, one, 0)


def main_kernel(
    pos_ref, dir_ref, arrived_ref, sums_in_ref,
    return_ref, terms_ref,
    rows_ref, cols_ref, left_ref, center_ref, sums_ref, list_ref, table_ref, sem,
):
    peers = arrived_ref.shape[0] // MSG
    marks = arrived_ref[pl.ds(RET, peers, stride=MSG), :].astype(BF16)
    pick = (
        lax.broadcasted_iota(jnp.int32, (16, LANES), 0)
        == lax.broadcasted_iota(jnp.int32, (16, LANES), 1)
    ).astype(BF16)
    found = lax.dot_general(pick, marks, NT, preferred_element_type=F32)
    wide = jnp.concatenate([found[0:1], found[1:2]], axis=1)
    slots = 2 * peers
    valid = wide >= 0.0
    slot = lax.broadcasted_iota(jnp.int32, (1, slots), 1)
    before = (
        lax.broadcasted_iota(jnp.int32, (slots, slots), 0)
        < lax.broadcasted_iota(jnp.int32, (slots, slots), 1)
    ).astype(BF16)
    ones = jnp.broadcast_to(valid.astype(F32), (16, slots)).astype(BF16)
    place = lax.dot_general(ones, before, NN, preferred_element_type=F32)[0:1]
    hot = (lax.broadcasted_iota(jnp.int32, (slots, slots), 0).astype(F32) == place) & valid
    row = lax.broadcasted_iota(jnp.int32, (16, slots), 0)
    codes = jnp.where(
        row == 0,
        jnp.broadcast_to(wide, (16, slots)),
        jnp.where(row == 1, jnp.broadcast_to(slot, (16, slots)).astype(F32), 0.0),
    ).astype(BF16)
    ordered = lax.dot_general(codes, hot.astype(F32).astype(BF16), NT, preferred_element_type=F32)
    total = jnp.sum(valid.astype(F32), axis=1, keepdims=True)
    ordered = jnp.where(
        lax.broadcasted_iota(jnp.int32, (8, slots), 0) == 2, total, ordered[:8]
    )
    list_ref[:, :slots] = ordered.astype(jnp.int32)
    copy = pltpu.make_async_copy(list_ref, table_ref, sem)
    copy.start()
    local_setup(pos_ref, dir_ref, rows_ref, cols_ref, left_ref, center_ref)
    sums_ref[...] = sums_in_ref[...]
    copy.wait()

    def one(pair, carry):
        block = table_ref[0, pair]
        where = table_ref[1, pair]
        second = (where >= peers).astype(jnp.int32)
        peer = where - second * peers
        remote, local = one_pair(
            block,
            eight_rows(arrived_ref[pl.ds(peer * MSG + second * 6, 6), :]),
            cols_ref, left_ref, center_ref,
        )
        return_ref[pl.ds(peer * RET + second * 6, 6), :] = remote[:6]
        sums_ref[block] += local
        return carry

    lax.fori_loop(0, table_ref[2, 0], one, 0)
    for block in range(terms_ref.shape[0]):
        terms_ref[block] = own_terms(rows_ref[block], sums_ref[block])


def finish_kernel(
    local_ref, slot_ref, count_ref, face_ref, returned_ref, terms_ref, back_ref,
    grad_ref, hess_ref,
    total_ref,
):
    total_ref[...] = terms_ref[...]
    for face in range(face_ref.shape[0]):
        total_ref[face_ref[face], 0:6, :] += back_ref[face * 6 : face * 6 + 6, :]

    def one(pair, carry):
        total_ref[local_ref[pair], 0:6, :] += returned_ref[pl.ds(slot_ref[pair], 6), :]
        return carry

    lax.fori_loop(0, count_ref[0], one, 0)
    for block in range(terms_ref.shape[0]):
        span = slice(block * LANES, (block + 1) * LANES)
        grad_ref[:, span] = total_ref[block, 0:3, :]
        hess_ref[:, span] = total_ref[block, 3:6, :]


def smem():
    return pl.BlockSpec(memory_space=pltpu.SMEM)


def vmem():
    return pl.BlockSpec(memory_space=pltpu.VMEM)


def shaped(*shape, dtype=F32):
    return jax.ShapeDtypeStruct(shape, dtype)


def per_device(
    positions, direction, pair_local, pair_peer, pair_shift, pair_count,
    face_index, cross_local, cross_face,
):
    num_blocks = positions.shape[1] // LANES
    peers = lax.axis_size("blk")
    faces = face_index.shape[0]
    setup = [
        pltpu.VMEM((num_blocks, 8, LANES), F32),
        pltpu.VMEM((num_blocks, LANES, 8), F32),
        pltpu.VMEM((num_blocks, 32, 2 * LANES), BF16),
        pltpu.VMEM((num_blocks, 8, LANES), F32),
    ]
    send, face_rows, slots = pl.pallas_call(
        pack_kernel,
        name="pack",
        out_shape=(
            shaped(peers * MSG, LANES),
            shaped(faces * 6, LANES),
            shaped(pair_local.shape[0], dtype=jnp.int32),
        ),
        in_specs=[smem()] * 5 + [vmem()] * 2,
        out_specs=(vmem(), vmem(), smem()),
        scratch_shapes=[pltpu.SMEM((peers,), jnp.int32)],
    )(pair_local, pair_peer, pair_shift, pair_count, face_index, positions, direction)
    arrived = lax.all_to_all(
        send.reshape(peers, MSG, 1, LANES), "blk", split_axis=0, concat_axis=0, tiled=True
    ).reshape(peers * MSG, LANES)
    incoming = from_behind(face_rows, "body", 1)
    sums, back = pl.pallas_call(
        cross_kernel,
        name="cross",
        out_shape=(shaped(num_blocks, 8, 2 * LANES), shaped(faces * 6, LANES)),
        in_specs=[smem()] * 2 + [vmem()] * 3,
        out_specs=(vmem(), vmem()),
        scratch_shapes=setup,
    )(cross_local, cross_face, positions, direction, incoming)
    face_back = from_behind(back, "body", -1)
    outgoing, terms = pl.pallas_call(
        main_kernel,
        name="pairs",
        out_shape=(shaped(peers * RET, LANES), shaped(num_blocks, 8, LANES)),
        in_specs=[vmem()] * 4,
        out_specs=(vmem(), vmem()),
        scratch_shapes=setup
        + [
            pltpu.VMEM((num_blocks, 8, 2 * LANES), F32),
            pltpu.VMEM((8, LANES), jnp.int32),
            pltpu.SMEM((8, LANES), jnp.int32),
            pltpu.SemaphoreType.DMA,
        ],
    )(positions, direction, arrived, sums)
    returned = lax.all_to_all(
        outgoing.reshape(peers, RET, 1, LANES), "blk", split_axis=0, concat_axis=0, tiled=True
    ).reshape(peers * RET, LANES)
    return pl.pallas_call(
        finish_kernel,
        name="finish",
        out_shape=(shaped(3, num_blocks * LANES), shaped(3, num_blocks * LANES)),
        in_specs=[smem()] * 4 + [vmem()] * 3,
        out_specs=(vmem(), vmem()),
        scratch_shapes=[pltpu.VMEM((num_blocks, 8, LANES), F32)],
    )(pair_local, slots, pair_count, face_index, returned, terms, face_back)


def solution(mesh):
    split = P(("blk", "body"))
    wide = P(None, ("blk", "body"))
    return jax.shard_map(
        per_device,
        mesh=mesh,
        in_specs=(wide, wide) + (split,) * 7,
        out_specs=(wide, wide),
        check_vma=False,
    )
```

```python
import jax
import jax.numpy as jnp
from jax import lax
from jax.experimental import pallas as pl
from jax.experimental.pallas import tpu as pltpu
from jax.sharding import PartitionSpec as P

XI = 0.1
SCALE = -0.04
GROUP = 4
LANES = 128
MSG = 13
RET = 12
F32 = jnp.float32
BF16 = jnp.bfloat16
NN = (((1,), (0,)), ((), ()))
NT = (((1,), (1,)), ((), ()))


def from_behind(value, axis, steps):
    count = lax.axis_size(axis)
    first, last = (max(0, -steps), min(count, count - steps))
    return lax.ppermute(value, axis, [(source, source + steps) for source in range(first, last)])


def block_rows(pos_ref, dir_ref, block):
    cols = pl.ds(pl.multiple_of(block * LANES, LANES), LANES)
    return pos_ref[:, cols], dir_ref[:, cols]


def pack_kernel(
    local_ref, peer_ref, shift_ref, count_ref, face_ref, pos_ref, dir_ref,
    send_ref, faces_ref, slot_ref, used_ref,
):
    peers = used_ref.shape[0]
    num_blocks = pos_ref.shape[1] // LANES
    lane = lax.broadcasted_iota(jnp.int32, (1, LANES), 1)
    unused = jnp.full((1, LANES), -1.0, F32)
    for face in range(face_ref.shape[0]):
        near_pos, near_dir = block_rows(pos_ref, dir_ref, face_ref[face])
        faces_ref[face * 6 : face * 6 + 3, :] = near_pos
        faces_ref[face * 6 + 3 : face * 6 + 6, :] = near_dir
    for peer in range(peers):
        used_ref[peer] = 0
        row = peer * MSG + RET
        send_ref[row : row + 1, :] = unused

    def one(pair, carry):
        near = local_ref[pair]
        peer = peer_ref[pair]
        far = lax.rem(near + shift_ref[pair], num_blocks)
        rank = used_ref[peer]
        used_ref[peer] = rank + 1
        slot_ref[pair] = peer * RET + rank * 6
        near_pos, near_dir = block_rows(pos_ref, dir_ref, near)
        base = peer * MSG
        send_ref[pl.ds(base + rank * 6, 3), :] = near_pos
        send_ref[pl.ds(base + rank * 6 + 3, 3), :] = near_dir
        row = pl.ds(base + RET, 1)
        send_ref[row, :] = jnp.where(lane == rank, far.astype(F32), send_ref[row, :])
        return carry

    lax.fori_loop(0, count_ref[0], one, 0)


def pieces(value):
    high = value.astype(BF16).astype(F32)
    rest = value - high
    mid = rest.astype(BF16).astype(F32)
    return high, mid, rest - mid


def own_terms(rows, sums):
    row = lax.broadcasted_iota(jnp.int32, (8, LANES), 0)
    by_grad = sums[:, :LANES]
    by_curv = sums[:, LANES:]
    first = rows * by_grad[6:7, :] - by_grad
    second = rows * by_curv[6:7, :] - by_curv
    shifted = pltpu.roll(second, 3, 0)
    return SCALE * (first + jnp.where((row >= 3) & (row < 6), shifted, 0.0))


def fold(product):
    return product[0:8] + product[8:16] + product[16:24]


def stacked(rows):
    row = lax.broadcasted_iota(jnp.int32, (8, LANES), 0)
    high, mid, low = pieces(jnp.where(row < 6, rows, jnp.where(row == 6, 1.0, 0.0)))
    tall = jnp.concatenate([high, mid, low, jnp.zeros_like(low)], axis=0).astype(BF16)
    return jnp.concatenate([tall, tall], axis=1)


def local_setup(pos_ref, dir_ref, rows_ref, feature_ref, left_ref, center_ref):
    row = lax.broadcasted_iota(jnp.int32, (8, LANES), 0)
    for block in range(pos_ref.shape[1] // LANES):
        span = slice(block * LANES, (block + 1) * LANES)
        rows = jnp.concatenate(
            [pos_ref[:, span], dir_ref[:, span], jnp.zeros((2, LANES), F32)], axis=0
        )
        center = jnp.mean(rows, axis=1, keepdims=True)
        rows = rows - center
        center_ref[block] = jnp.broadcast_to(center, (8, LANES))
        rows_ref[block] = jnp.where(row == 6, 1.0, rows)
        left_ref[block] = stacked(rows)
        square = jnp.sum(rows[0:3] * rows[0:3], axis=0, keepdims=True)
        cross = jnp.sum(rows[0:3] * rows[3:6], axis=0, keepdims=True)
        full = jnp.where(row == 6, square, jnp.where(row == 7, cross + cross, rows))
        high, mid, low = pieces(full)
        one = jnp.ones_like(full)
        feature_ref[block] = jnp.concatenate(
            [high, high, mid, high, mid, low, one, jnp.zeros_like(one)], axis=0
        ).T.astype(BF16)


def remote_feature(rows):
    row = lax.broadcasted_iota(jnp.int32, (8, LANES), 0)
    twice = -2.0 * rows
    for_square = jnp.where(row < 3, twice, jnp.where(row == 6, 1.0, 0.0))
    swapped = jnp.where(row < 3, pltpu.roll(twice, 5, 0), pltpu.roll(twice, 3, 0))
    for_cross = jnp.where(row < 6, swapped, jnp.where(row == 7, 1.0, 0.0))
    square = jnp.sum(rows[0:3] * rows[0:3], axis=0, keepdims=True) + XI
    cross = jnp.sum(rows[0:3] * twice[3:6], axis=0, keepdims=True)
    high, mid, low = pieces(jnp.concatenate([for_square, for_cross], axis=1))
    own = jnp.concatenate([square, -cross], axis=1)
    own_high, own_mid, own_low = pieces(own)
    wide_row = lax.broadcasted_iota(jnp.int32, (8, 2 * LANES), 0)
    norms = jnp.where(
        wide_row == 0, own_high,
        jnp.where(wide_row == 1, own_mid, jnp.where(wide_row == 2, own_low, 0.0)),
    )
    return jnp.concatenate(
        [high, mid, high, low, mid, high, norms, jnp.zeros_like(norms)], axis=0
    ).astype(BF16)


def split(value):
    high = value.astype(BF16)
    return high, (value - high.astype(F32)).astype(BF16)


def pair_group(blocks, remotes, feature_ref, left_ref, center_ref):
    remotes = [remote - center_ref[block] for block, remote in zip(blocks, remotes)]
    both = [
        lax.dot_general(
            feature_ref[block], remote_feature(remote), NN, preferred_element_type=F32
        )
        for block, remote in zip(blocks, remotes)
    ]
    results = []
    row = lax.broadcasted_iota(jnp.int32, (8, LANES), 0)
    for block, remote, product in zip(blocks, remotes, both):
        squared = jnp.minimum(product[:, :LANES], 1.0)
        along = product[:, LANES:]
        log_twice = 2.0 * jnp.log(squared)
        excess = squared - 1.0
        ratio = excess / squared
        grad_high, grad_low = split(excess * (log_twice + ratio))
        curv_high, curv_low = split((log_twice + ratio * (4.0 - ratio)) * along)
        by_local = jnp.concatenate(
            [
                jnp.concatenate([grad_high, curv_high], axis=1),
                jnp.concatenate([grad_low, curv_low], axis=1),
            ],
            axis=0,
        )
        by_remote = jnp.concatenate(
            [
                jnp.concatenate([grad_high, grad_low], axis=1),
                jnp.concatenate([curv_high, curv_low], axis=1),
            ],
            axis=0,
        )
        for_remote = lax.dot_general(left_ref[block], by_local, NN, preferred_element_type=F32)
        for_local = lax.dot_general(stacked(remote), by_remote, NT, preferred_element_type=F32)
        remote_rows = jnp.where(row == 6, 1.0, remote)
        results.append((own_terms(remote_rows, fold(for_remote)), fold(for_local)))
    return results


def eight_rows(six):
    return jnp.concatenate([six, jnp.zeros((2, LANES), F32)], axis=0)


def cross_kernel(
    local_ref, face_ref, pos_ref, dir_ref, incoming_ref,
    sums_ref, back_ref, rows_ref, feature_ref, left_ref, center_ref,
):
    local_setup(pos_ref, dir_ref, rows_ref, feature_ref, left_ref, center_ref)
    sums_ref[...] = jnp.zeros_like(sums_ref)
    back_ref[...] = jnp.zeros_like(back_ref)

    def some(step, carry):
        pairs = [step * GROUP + k for k in range(GROUP)]
        blocks = [local_ref[pair] for pair in pairs]
        rows = [pl.ds(face_ref[pair] * 6, 6) for pair in pairs]
        remotes = [eight_rows(incoming_ref[row, :]) for row in rows]
        results = pair_group(blocks, remotes, feature_ref, left_ref, center_ref)
        for block, row, (remote, local) in zip(blocks, rows, results):
            back_ref[row, :] += remote[:6]
            sums_ref[block] += local
        return carry

    count = jnp.where(lax.axis_index("body") > 0, local_ref.shape[0] // GROUP, 0)
    lax.fori_loop(0, count, some, 0)


def main_kernel(
    arrived_ref, sums_in_ref, rows_ref, feature_ref, left_ref, center_ref,
    return_ref, terms_ref,
    sums_ref, list_ref, table_ref, sem,
):
    peers = arrived_ref.shape[0] // MSG
    marks = arrived_ref[pl.ds(RET, peers, stride=MSG), :].astype(BF16)
    pick = (
        lax.broadcasted_iota(jnp.int32, (16, LANES), 0)
        == lax.broadcasted_iota(jnp.int32, (16, LANES), 1)
    ).astype(BF16)
    found = lax.dot_general(pick, marks, NT, preferred_element_type=F32)
    wide = jnp.concatenate([found[0:1], found[1:2]], axis=1)
    slots = 2 * peers
    valid = wide >= 0.0
    slot = lax.broadcasted_iota(jnp.int32, (1, slots), 1)
    before = (
        lax.broadcasted_iota(jnp.int32, (slots, slots), 0)
        < lax.broadcasted_iota(jnp.int32, (slots, slots), 1)
    ).astype(BF16)
    ones = jnp.broadcast_to(valid.astype(F32), (16, slots)).astype(BF16)
    place = lax.dot_general(ones, before, NN, preferred_element_type=F32)[0:1]
    hot = (lax.broadcasted_iota(jnp.int32, (slots, slots), 0).astype(F32) == place) & valid
    row = lax.broadcasted_iota(jnp.int32, (16, slots), 0)
    codes = jnp.where(
        row == 0,
        jnp.broadcast_to(wide, (16, slots)),
        jnp.where(row == 1, jnp.broadcast_to(slot, (16, slots)).astype(F32), 0.0),
    ).astype(BF16)
    ordered = lax.dot_general(codes, hot.astype(F32).astype(BF16), NT, preferred_element_type=F32)
    total = jnp.sum(valid.astype(F32), axis=1, keepdims=True)
    ordered = jnp.where(
        lax.broadcasted_iota(jnp.int32, (8, slots), 0) == 2, total, ordered[:8]
    )
    list_ref[:, :slots] = ordered.astype(jnp.int32)
    copy = pltpu.make_async_copy(list_ref, table_ref, sem)
    copy.start()
    num_blocks = terms_ref.shape[0]
    sums_ref[0:num_blocks] = sums_in_ref[...]
    sums_ref[num_blocks] = jnp.zeros((8, 2 * LANES), F32)
    copy.wait()
    count = table_ref[2, 0]

    def some(step, carry):
        blocks, targets, remotes, rows = [], [], [], []
        for k in range(GROUP):
            pair = step * GROUP + k
            listed = jnp.minimum(pair, count - 1)
            block = table_ref[0, listed]
            where = table_ref[1, listed]
            second = (where >= peers).astype(jnp.int32)
            peer = where - second * peers
            blocks.append(block)
            targets.append(jnp.where(pair < count, block, num_blocks))
            remotes.append(eight_rows(arrived_ref[pl.ds(peer * MSG + second * 6, 6), :]))
            rows.append(pl.ds(peer * RET + second * 6, 6))
        results = pair_group(blocks, remotes, feature_ref, left_ref, center_ref)
        for target, row, (remote, local) in zip(targets, rows, results):
            return_ref[row, :] = remote[:6]
            sums_ref[target] += local
        return carry

    lax.fori_loop(0, (count + GROUP - 1) // GROUP, some, 0)
    for block in range(terms_ref.shape[0]):
        terms_ref[block] = own_terms(rows_ref[block], sums_ref[block])


def finish_kernel(
    local_ref, slot_ref, count_ref, face_ref, returned_ref, terms_ref, back_ref,
    grad_ref, hess_ref,
    total_ref,
):
    total_ref[...] = terms_ref[...]
    for face in range(face_ref.shape[0]):
        total_ref[face_ref[face], 0:6, :] += back_ref[face * 6 : face * 6 + 6, :]

    def one(pair, carry):
        total_ref[local_ref[pair], 0:6, :] += returned_ref[pl.ds(slot_ref[pair], 6), :]
        return carry

    lax.fori_loop(0, count_ref[0], one, 0)
    for block in range(terms_ref.shape[0]):
        span = slice(block * LANES, (block + 1) * LANES)
        grad_ref[:, span] = total_ref[block, 0:3, :]
        hess_ref[:, span] = total_ref[block, 3:6, :]


def smem():
    return pl.BlockSpec(memory_space=pltpu.SMEM)


def vmem():
    return pl.BlockSpec(memory_space=pltpu.VMEM)


def on_chip(*shape, dtype=F32):
    return pltpu.VMEM(shape, dtype)


def held(*values):
    return [pltpu.with_memory_space_constraint(value, pltpu.VMEM) for value in values]


def per_device(
    positions, direction, pair_local, pair_peer, pair_shift, pair_count,
    face_index, cross_local, cross_face,
):
    num_blocks = positions.shape[1] // LANES
    peers = lax.axis_size("blk")
    faces = face_index.shape[0]
    setup = (
        on_chip(num_blocks, 8, LANES),
        on_chip(num_blocks, LANES, 64, dtype=BF16),
        on_chip(num_blocks, 32, 2 * LANES, dtype=BF16),
        on_chip(num_blocks, 8, LANES),
    )
    send, face_rows, slots = pl.pallas_call(
        pack_kernel,
        name="pack",
        out_shape=(
            on_chip(peers * MSG, LANES),
            on_chip(faces * 6, LANES),
            pltpu.SMEM((pair_local.shape[0],), jnp.int32),
        ),
        in_specs=[smem()] * 5 + [vmem()] * 2,
        out_specs=(vmem(), vmem(), smem()),
        scratch_shapes=[pltpu.SMEM((peers,), jnp.int32)],
    )(pair_local, pair_peer, pair_shift, pair_count, face_index, positions, direction)
    arrived = lax.all_to_all(
        send.reshape(peers, MSG, 1, LANES), "blk", split_axis=0, concat_axis=0, tiled=True
    ).reshape(peers * MSG, LANES)
    incoming = from_behind(face_rows, "body", 1)
    sums, back, *local = pl.pallas_call(
        cross_kernel,
        name="cross",
        out_shape=(on_chip(num_blocks, 8, 2 * LANES), on_chip(faces * 6, LANES)) + setup,
        in_specs=[smem()] * 2 + [vmem()] * 3,
        out_specs=(vmem(),) * 6,
    )(cross_local, cross_face, positions, direction, *held(incoming))
    face_back = from_behind(back, "body", -1)
    outgoing, terms = pl.pallas_call(
        main_kernel,
        name="pairs",
        out_shape=(on_chip(peers * RET, LANES), on_chip(num_blocks, 8, LANES)),
        in_specs=[vmem()] * 6,
        out_specs=(vmem(), vmem()),
        scratch_shapes=[
            pltpu.VMEM((num_blocks + 1, 8, 2 * LANES), F32),
            pltpu.VMEM((8, LANES), jnp.int32),
            pltpu.SMEM((8, LANES), jnp.int32),
            pltpu.SemaphoreType.DMA,
        ],
    )(*held(arrived, sums, *local))
    returned = lax.all_to_all(
        outgoing.reshape(peers, RET, 1, LANES), "blk", split_axis=0, concat_axis=0, tiled=True
    ).reshape(peers * RET, LANES)
    return pl.pallas_call(
        finish_kernel,
        name="finish",
        out_shape=[jax.ShapeDtypeStruct((3, num_blocks * LANES), F32)] * 2,
        in_specs=[smem()] * 4 + [vmem()] * 3,
        out_specs=(vmem(), vmem()),
        scratch_shapes=[pltpu.VMEM((num_blocks, 8, LANES), F32)],
    )(pair_local, slots, pair_count, face_index, *held(returned, terms, face_back))


def solution(mesh):
    split = P(("blk", "body"))
    wide = P(None, ("blk", "body"))
    return jax.shard_map(
        per_device,
        mesh=mesh,
        in_specs=(wide, wide) + (split,) * 7,
        out_specs=(wide, wide),
        check_vma=False,
    )
```

```python
import jax
import jax.numpy as jnp
from jax import lax
from jax.experimental import pallas as pl
from jax.experimental.pallas import tpu as pltpu
from jax.sharding import PartitionSpec as P

XI = 0.1
SCALE = 0.02
LANES = 128
SIX = 6
MSG = 13
RET = 12
GROUP = 3
UNROLL = 4
F32 = jnp.float32
BF16 = jnp.bfloat16
NN = (((1,), (0,)), ((), ()))
NT = (((1,), (1,)), ((), ()))


def from_behind(value, axis, steps):
    count = lax.axis_size(axis)
    first, last = (max(0, -steps), min(count, count - steps))
    return lax.ppermute(value, axis, [(source, source + steps) for source in range(first, last)])


def put_block(target_ref, start, pos_ref, dir_ref, block):
    cols = pl.ds(pl.multiple_of(block * LANES, LANES), LANES)
    target_ref[pl.ds(start, 3), :] = pos_ref[:, cols]
    target_ref[pl.ds(start + 3, 3), :] = dir_ref[:, cols]


def pack_kernel(
    local_ref, peer_ref, shift_ref, count_ref, face_ref, pos_ref, dir_ref,
    send_ref, faces_ref, plan_ref, used_ref,
):
    peers = used_ref.shape[0]
    pairs = local_ref.shape[0]
    num_blocks = pos_ref.shape[1] // LANES
    count = count_ref[0]
    lane = lax.broadcasted_iota(jnp.int32, (1, LANES), 1)
    unused = jnp.full((1, LANES), -1.0, F32)
    for peer in range(peers):
        used_ref[peer] = 0
        row = peer * MSG + RET
        send_ref[row : row + 1, :] = unused

    def some(step, carry):
        for k in range(UNROLL):
            pair = step * UNROLL + k
            near = local_ref[pair]
            peer = peer_ref[pair]
            far = lax.rem(near + shift_ref[pair], num_blocks)
            mark = jnp.where(pair < count, far, -1).astype(F32)
            rank = used_ref[peer]
            used_ref[peer] = rank + 1
            plan_ref[pair] = peer * RET + rank * SIX
            plan_ref[pairs + pair] = near
            put_block(send_ref, peer * MSG + rank * SIX, pos_ref, dir_ref, near)
            pltpu.store(
                send_ref.at[pl.ds(peer * MSG + RET, 1), :],
                jnp.broadcast_to(mark, (1, LANES)),
                mask=lane == rank,
            )
        return carry

    lax.fori_loop(0, (count + UNROLL - 1) // UNROLL, some, 0)
    plan_ref[2 * pairs] = count
    for face in range(face_ref.shape[0]):
        block = face_ref[face]
        plan_ref[2 * pairs + 1 + face] = block
        put_block(faces_ref, face * SIX, pos_ref, dir_ref, block)


def pieces(value):
    high = value.astype(BF16).astype(F32)
    rest = value - high
    mid = rest.astype(BF16).astype(F32)
    return high, mid, rest - mid


def own_terms(rows, sums):
    row = lax.broadcasted_iota(jnp.int32, (8, LANES), 0)
    by_grad = sums[:, :LANES]
    by_curv = sums[:, LANES:]
    first = rows * by_grad[6:7, :] - by_grad
    second = rows * by_curv[6:7, :] - by_curv
    shifted = pltpu.roll(second, 3, 0)
    return first + jnp.where((row >= 3) & (row < 6), shifted, 0.0)


def fold(product):
    return product[0:8] + product[8:16] + product[16:24]


def twice_wide(tall):
    return jnp.concatenate([tall, tall], axis=1)


def remote_operands(rows):
    row = lax.broadcasted_iota(jnp.int32, (8, LANES), 0)
    twice = jnp.where(row == 6, -2.0, -2.0 * rows)
    high, mid, low = pieces(twice)
    products = twice * jnp.where(row < 3, twice, pltpu.roll(twice, 3, 0))
    p_high, p_mid, p_low = pieces(products)
    zero = jnp.zeros_like(low)
    high_mid = jnp.concatenate([high, mid], axis=0).astype(BF16)
    high_low = jnp.concatenate([high, low], axis=0).astype(BF16)
    low_zero = jnp.concatenate([low, zero], axis=0).astype(BF16)
    p_high_mid = jnp.concatenate([p_high, p_mid], axis=0).astype(BF16)
    p_low_zero = jnp.concatenate([p_low, zero], axis=0).astype(BF16)
    distances = jnp.concatenate([high_mid, high_mid, high_low, p_high_mid, p_low_zero], axis=0)
    return distances, jnp.concatenate([high_mid, low_zero], axis=0)


def local_operands(rows):
    row = lax.broadcasted_iota(jnp.int32, (8, LANES), 0)
    square = jnp.sum(rows[0:3] * rows[0:3], axis=0, keepdims=True) + XI
    cross = jnp.sum(rows[0:3] * rows[3:6], axis=0, keepdims=True)
    for_square = jnp.where(row < 3, rows, jnp.where(row == 6, -0.5 * square, 0.0))
    swapped = jnp.where(row < 3, pltpu.roll(rows, 5, 0), pltpu.roll(rows, 3, 0))
    for_cross = jnp.where(row < 6, swapped, jnp.where(row == 6, -cross, 0.0))
    squares = jnp.where(row < 3, 0.25, jnp.zeros_like(rows))
    crosses = jnp.where((row >= 3) & (row < 6), 0.5, jnp.zeros_like(rows))
    halves = []
    for full, own in ((for_square, squares), (for_cross, crosses)):
        high, mid, low = pieces(full)
        tall = [high, high, mid, mid, low, high, own, own, own, jnp.zeros_like(own)]
        tall += [jnp.zeros_like(own)] * 6
        halves.append(jnp.concatenate(tall, axis=0).T)
    return jnp.concatenate(halves, axis=0).astype(BF16)


def local_setup(pos_ref, dir_ref, rows_ref, feature_ref, left_ref, center_ref):
    row = lax.broadcasted_iota(jnp.int32, (8, LANES), 0)
    for block in range(pos_ref.shape[1] // LANES):
        span = slice(block * LANES, (block + 1) * LANES)
        rows = jnp.concatenate(
            [pos_ref[:, span], dir_ref[:, span], jnp.zeros((2, LANES), F32)], axis=0
        )
        center = jnp.mean(rows, axis=1, keepdims=True)
        rows = rows - center
        center_ref[block] = jnp.broadcast_to(center, (8, LANES))
        rows_ref[block] = rows
        feature_ref[block] = local_operands(rows)
        left_ref[block] = twice_wide(remote_operands(rows)[1])


def split(value):
    high = value.astype(BF16)
    return high, (value - high.astype(F32)).astype(BF16)


def pair_coefficients(product):
    squared = jnp.minimum(product[:LANES], 1.0)
    along = product[LANES:]
    log_ratio = jnp.log(squared)
    log_twice = log_ratio + log_ratio
    excess = squared - 1.0
    ratio = excess / squared
    return (
        split(excess * (log_twice + ratio)),
        split((log_twice + ratio * (4.0 - ratio)) * along),
    )


def pair_sums(grad, curv, left, right, remote):
    by_local = jnp.concatenate(
        [jnp.concatenate([grad[k], curv[k]], axis=1) for k in range(2)], axis=0
    )
    by_remote = jnp.concatenate(
        [jnp.concatenate([both[0], both[1]], axis=1) for both in (grad, curv)], axis=0
    )
    for_remote = lax.dot_general(left, by_local, NN, preferred_element_type=F32)
    for_local = lax.dot_general(twice_wide(right), by_remote, NT, preferred_element_type=F32)
    return own_terms(remote, fold(for_remote)), fold(for_local)


def eight_rows(six):
    return jnp.concatenate([six, jnp.zeros((2, LANES), F32)], axis=0)


def cross_kernel(
    local_ref, face_ref, pos_ref, dir_ref, incoming_ref,
    sums_ref, back_ref, rows_ref, feature_ref, left_ref, center_ref,
):
    local_setup(pos_ref, dir_ref, rows_ref, feature_ref, left_ref, center_ref)
    sums_ref[...] = jnp.zeros_like(sums_ref)
    back_ref[...] = jnp.zeros_like(back_ref)

    def some(step, carry):
        pairs = [step * 4 + k for k in range(4)]
        blocks = [local_ref[pair] for pair in pairs]
        rows = [pl.ds(face_ref[pair] * SIX, SIX) for pair in pairs]
        remotes = [
            eight_rows(incoming_ref[row, :]) - center_ref[block] for block, row in zip(blocks, rows)
        ]
        operands = [remote_operands(remote) for remote in remotes]
        products = [
            lax.dot_general(
                feature_ref[block, :, : right.shape[0]], right, NN, preferred_element_type=F32
            )
            for block, (right, _) in zip(blocks, operands)
        ]
        for block, row, remote, (_, right), product in zip(
            blocks, rows, remotes, operands, products
        ):
            grad, curv = pair_coefficients(product)
            remote, local = pair_sums(grad, curv, left_ref[block], right, remote)
            back_ref[row, :] += remote[:SIX]
            sums_ref[block] += local
        return carry

    count = jnp.where(lax.axis_index("body") > 0, local_ref.shape[0] // 4, 0)
    lax.fori_loop(0, count, some, 0)


def main_kernel(
    arrived_ref, sums_in_ref, rows_ref, feature_ref, left_ref, center_ref,
    return_ref, terms_ref,
    sums_ref, list_ref, table_ref, sem,
    dist_a, dist_b, right_a, right_b, remote_a, remote_b,
):
    peers = arrived_ref.shape[0] // MSG
    slots = 2 * peers
    num_blocks = terms_ref.shape[0]
    marks = arrived_ref[pl.ds(RET, peers, stride=MSG), :].astype(BF16)
    pick = (
        lax.broadcasted_iota(jnp.int32, (16, LANES), 0)
        == lax.broadcasted_iota(jnp.int32, (16, LANES), 1)
    ).astype(BF16)
    found = lax.dot_general(pick, marks, NT, preferred_element_type=F32)
    wide = jnp.concatenate([found[0:1], found[1:2]], axis=1)
    valid = wide >= 0.0
    slot = lax.broadcasted_iota(jnp.int32, (1, slots), 1)
    one = lax.broadcasted_iota(jnp.int32, (slots, slots), 0)
    before = (one < lax.broadcasted_iota(jnp.int32, (slots, slots), 1)).astype(BF16)
    ones = jnp.broadcast_to(valid.astype(F32), (16, slots)).astype(BF16)
    place = lax.dot_general(ones, before, NN, preferred_element_type=F32)[0:1]
    hot = (one.astype(F32) == place) & valid
    row = lax.broadcasted_iota(jnp.int32, (16, slots), 0)
    second = slot >= peers
    peer = jnp.where(second, slot - peers, slot).astype(F32)
    codes = jnp.where(row == 0, jnp.broadcast_to(wide, (16, slots)), 0.0)
    codes = jnp.where(row == 1, jnp.broadcast_to(peer, (16, slots)), codes)
    codes = jnp.where(row == 2, jnp.broadcast_to(second.astype(F32), (16, slots)), codes)
    ordered = lax.dot_general(
        codes.astype(BF16), hot.astype(F32).astype(BF16), NT, preferred_element_type=F32
    )
    ordered = ordered[:8].astype(jnp.int32)
    total = jnp.sum(valid.astype(F32), axis=1, keepdims=True).astype(jnp.int32)
    row = row[:8]
    base = ordered[1:2]
    shift = ordered[2:3] * SIX
    table = jnp.where(row == 0, ordered[0:1], 0)
    table = jnp.where(row == 1, base * MSG + shift, table)
    table = jnp.where(row == 2, base * RET + shift, table)
    list_ref[:, :slots] = jnp.where(row == 3, total, table)
    copy = pltpu.make_async_copy(list_ref, table_ref, sem)
    copy.start()
    sums_ref[0:num_blocks] = sums_in_ref[...]
    sums_ref[num_blocks] = jnp.zeros((8, 2 * LANES), F32)
    copy.wait()
    count = table_ref[3, 0]

    def listed(group, k):
        return jnp.clip(group * GROUP + k, 0, count - 1)

    def distances(group, dist_ref, right_ref, remote_ref):
        for k in range(GROUP):
            pair = listed(group, k)
            block = table_ref[0, pair]
            rows = eight_rows(arrived_ref[pl.ds(table_ref[1, pair], SIX), :]) - center_ref[block]
            right, sums_right = remote_operands(rows)
            remote_ref[k] = rows
            right_ref[k] = sums_right
            dist_ref[k] = lax.dot_general(
                feature_ref[block, :, : right.shape[0]], right, NN, preferred_element_type=F32
            )

    def sums(group, dist_ref, right_ref, remote_ref):
        for k in range(GROUP):
            pair = group * GROUP + k
            known = listed(group, k)
            block = table_ref[0, known]
            target = jnp.where(pair < count, block, num_blocks)
            grad, curv = pair_coefficients(dist_ref[k])
            remote, local = pair_sums(grad, curv, left_ref[block], right_ref[k], remote_ref[k])
            return_ref[pl.ds(table_ref[2, known], SIX), :] = remote[:SIX]
            sums_ref[target] += local

    def two_groups(step, carry):
        group = 2 * step
        distances(group + 1, dist_b, right_b, remote_b)
        sums(group, dist_a, right_a, remote_a)
        distances(group + 2, dist_a, right_a, remote_a)
        sums(group + 1, dist_b, right_b, remote_b)
        return carry

    @pl.when(count > 0)
    def _():
        distances(0, dist_a, right_a, remote_a)
        lax.fori_loop(0, (count + 2 * GROUP - 1) // (2 * GROUP), two_groups, 0)

    for block in range(num_blocks):
        terms_ref[block] = own_terms(rows_ref[block], sums_ref[block])


def finish_kernel(
    plan_ref, returned_ref, terms_ref, back_ref,
    grad_ref, hess_ref,
    total_ref,
):
    num_blocks = terms_ref.shape[0]
    faces = back_ref.shape[0] // SIX
    pairs = (plan_ref.shape[0] - 1 - faces) // 2
    total_ref[0:num_blocks] = terms_ref[...]
    for face in range(faces):
        block = plan_ref[2 * pairs + 1 + face]
        total_ref[block, 0:SIX, :] += back_ref[face * SIX : face * SIX + SIX, :]
    count = plan_ref[2 * pairs]

    def some(step, carry):
        for k in range(UNROLL):
            pair = step * UNROLL + k
            block = jnp.where(pair < count, plan_ref[pairs + pair], num_blocks)
            total_ref[block, 0:SIX, :] += returned_ref[pl.ds(plan_ref[pair], SIX), :]
        return carry

    lax.fori_loop(0, (count + UNROLL - 1) // UNROLL, some, 0)
    for block in range(num_blocks):
        span = slice(block * LANES, (block + 1) * LANES)
        grad_ref[:, span] = SCALE * total_ref[block, 0:3, :]
        hess_ref[:, span] = SCALE * total_ref[block, 3:6, :]


def smem():
    return pl.BlockSpec(memory_space=pltpu.SMEM)


def vmem():
    return pl.BlockSpec(memory_space=pltpu.VMEM)


def on_chip(*shape, dtype=F32):
    return pltpu.VMEM(shape, dtype)


def held(*values):
    return [pltpu.with_memory_space_constraint(value, pltpu.VMEM) for value in values]


def exchange(rows, peers):
    count = rows.shape[0] // peers
    return lax.all_to_all(
        rows.reshape(peers, count, 1, LANES), "blk", split_axis=0, concat_axis=0, tiled=True
    ).reshape(rows.shape)


def per_device(
    positions, direction, pair_local, pair_peer, pair_shift, pair_count,
    face_index, cross_local, cross_face,
):
    num_blocks = positions.shape[1] // LANES
    peers = lax.axis_size("blk")
    faces = face_index.shape[0]
    setup = (
        on_chip(num_blocks, 8, LANES),
        on_chip(num_blocks, 2 * LANES, LANES, dtype=BF16),
        on_chip(num_blocks, 32, 2 * LANES, dtype=BF16),
        on_chip(num_blocks, 8, LANES),
    )
    send, face_rows, plan = pl.pallas_call(
        pack_kernel,
        name="pack",
        out_shape=(
            on_chip(peers * MSG, LANES),
            on_chip(faces * SIX, LANES),
            pltpu.SMEM((2 * pair_local.shape[0] + 1 + faces,), jnp.int32),
        ),
        in_specs=[smem()] * 5 + [vmem()] * 2,
        out_specs=(vmem(), vmem(), smem()),
        scratch_shapes=[pltpu.SMEM((peers,), jnp.int32)],
    )(pair_local, pair_peer, pair_shift, pair_count, face_index, positions, direction)
    arrived = exchange(send, peers)
    incoming = from_behind(face_rows, "body", 1)
    sums, back, *local = pl.pallas_call(
        cross_kernel,
        name="cross",
        out_shape=(on_chip(num_blocks, 8, 2 * LANES), on_chip(faces * SIX, LANES)) + setup,
        in_specs=[smem()] * 2 + [vmem()] * 3,
        out_specs=(vmem(),) * 6,
    )(cross_local, cross_face, positions, direction, *held(incoming))
    face_back = from_behind(back, "body", -1)
    outgoing, terms = pl.pallas_call(
        main_kernel,
        name="pairs",
        out_shape=(on_chip(peers * RET, LANES), on_chip(num_blocks, 8, LANES)),
        in_specs=[vmem()] * 6,
        out_specs=(vmem(), vmem()),
        scratch_shapes=[
            pltpu.VMEM((num_blocks + 1, 8, 2 * LANES), F32),
            pltpu.VMEM((8, LANES), jnp.int32),
            pltpu.SMEM((8, LANES), jnp.int32),
            pltpu.SemaphoreType.DMA,
        ]
        + [pltpu.VMEM((GROUP, 2 * LANES, LANES), F32)] * 2
        + [pltpu.VMEM((GROUP, 32, LANES), BF16)] * 2
        + [pltpu.VMEM((GROUP, 8, LANES), F32)] * 2,
    )(*held(arrived, sums, *local))
    returned = exchange(outgoing, peers)
    return pl.pallas_call(
        finish_kernel,
        name="finish",
        out_shape=[jax.ShapeDtypeStruct((3, num_blocks * LANES), F32)] * 2,
        in_specs=[smem()] + [vmem()] * 3,
        out_specs=(vmem(), vmem()),
        scratch_shapes=[pltpu.VMEM((num_blocks + 1, 8, LANES), F32)],
    )(plan, *held(returned, terms, face_back))


def solution(mesh):
    split_all = P(("blk", "body"))
    wide = P(None, ("blk", "body"))
    return jax.shard_map(
        per_device,
        mesh=mesh,
        in_specs=(wide, wide) + (split_all,) * 7,
        out_specs=(wide, wide),
        check_vma=False,
    )
```

```python
import functools

import jax
import jax.numpy as jnp
from jax import lax
from jax.experimental import pallas as pl
from jax.experimental.pallas import tpu as pltpu
from jax.sharding import PartitionSpec as P

XI = 0.1
TWICE_LN2 = 1.3862943611198906
SCALE = 0.02
LANES = 128
SIX = 6
MSG = 13
RET = 12
GROUP = 3
IN_TURN = 3
UNROLL = 4
F32 = jnp.float32
BF16 = jnp.bfloat16
NN = (((1,), (0,)), ((), ()))
NT = (((1,), (1,)), ((), ()))


def from_behind(value, axis, steps):
    count = lax.axis_size(axis)
    first, last = (max(0, -steps), min(count, count - steps))
    return lax.ppermute(value, axis, [(source, source + steps) for source in range(first, last)])


def put_block(target_ref, start, pos_ref, dir_ref, block):
    cols = pl.ds(pl.multiple_of(block * LANES, LANES), LANES)
    target_ref[pl.ds(start, 3), :] = pos_ref[:, cols]
    target_ref[pl.ds(start + 3, 3), :] = dir_ref[:, cols]


def pack_kernel(
    local_ref, peer_ref, shift_ref, count_ref, face_ref, pos_ref, dir_ref,
    send_ref, faces_ref, plan_ref, used_ref,
):
    peers = used_ref.shape[0]
    pairs = local_ref.shape[0]
    num_blocks = pos_ref.shape[1] // LANES
    count = count_ref[0]
    lane = lax.broadcasted_iota(jnp.int32, (1, LANES), 1)
    unused = jnp.full((1, LANES), -1.0, F32)
    for peer in range(peers):
        used_ref[peer] = 0
        row = peer * MSG + RET
        send_ref[row : row + 1, :] = unused

    def some(step, carry):
        for k in range(UNROLL):
            pair = step * UNROLL + k
            near = local_ref[pair]
            peer = peer_ref[pair]
            far = lax.rem(near + shift_ref[pair], num_blocks)
            mark = jnp.where(pair < count, far, -1).astype(F32)
            rank = used_ref[peer]
            used_ref[peer] = rank + 1
            plan_ref[pair] = peer * RET + rank * SIX
            plan_ref[pairs + pair] = near
            put_block(send_ref, peer * MSG + rank * SIX, pos_ref, dir_ref, near)
            pltpu.store(
                send_ref.at[pl.ds(peer * MSG + RET, 1), :],
                jnp.broadcast_to(mark, (1, LANES)),
                mask=lane == rank,
            )
        return carry

    lax.fori_loop(0, (count + UNROLL - 1) // UNROLL, some, 0)
    plan_ref[2 * pairs] = count
    for face in range(face_ref.shape[0]):
        block = face_ref[face]
        plan_ref[2 * pairs + 1 + face] = block
        put_block(faces_ref, face * SIX, pos_ref, dir_ref, block)


def pieces(value):
    high = value.astype(BF16).astype(F32)
    rest = value - high
    mid = rest.astype(BF16).astype(F32)
    return high, mid, rest - mid


def own_terms(rows, sums):
    row = lax.broadcasted_iota(jnp.int32, (8, LANES), 0)
    by_grad = sums[:, :LANES]
    by_curv = sums[:, LANES:]
    first = rows * by_grad[6:7, :] - by_grad
    second = rows * by_curv[6:7, :] - by_curv
    shifted = pltpu.roll(second, 3, 0)
    return first + jnp.where((row >= 3) & (row < 6), shifted, 0.0)


def fold(product):
    return product[0:8] + product[8:16] + product[16:24]


def twice_wide(tall):
    return jnp.concatenate([tall, tall], axis=1)


def remote_operands(rows):
    row = lax.broadcasted_iota(jnp.int32, (8, LANES), 0)
    twice = jnp.where(row == 6, -2.0, -2.0 * rows)
    high, mid, low = pieces(twice)
    products = twice * jnp.where(row < 3, twice, pltpu.roll(twice, 3, 0))
    p_high, p_mid, p_low = pieces(products)
    zero = jnp.zeros_like(low)
    high_mid = jnp.concatenate([high, mid], axis=0).astype(BF16)
    high_low = jnp.concatenate([high, low], axis=0).astype(BF16)
    low_zero = jnp.concatenate([low, zero], axis=0).astype(BF16)
    p_high_mid = jnp.concatenate([p_high, p_mid], axis=0).astype(BF16)
    p_low_zero = jnp.concatenate([p_low, zero], axis=0).astype(BF16)
    distances = jnp.concatenate([high_mid, high_mid, high_low, p_high_mid, p_low_zero], axis=0)
    return distances, jnp.concatenate([high_mid, low_zero], axis=0)


def local_operands(rows):
    row = lax.broadcasted_iota(jnp.int32, (8, LANES), 0)
    square = jnp.sum(rows[0:3] * rows[0:3], axis=0, keepdims=True) + XI
    cross = jnp.sum(rows[0:3] * rows[3:6], axis=0, keepdims=True)
    for_square = jnp.where(row < 3, rows, jnp.where(row == 6, -0.5 * square, 0.0))
    swapped = jnp.where(row < 3, pltpu.roll(rows, 5, 0), pltpu.roll(rows, 3, 0))
    for_cross = jnp.where(row < 6, swapped, jnp.where(row == 6, -cross, 0.0))
    squares = jnp.where(row < 3, 0.25, jnp.zeros_like(rows))
    crosses = jnp.where((row >= 3) & (row < 6), 0.5, jnp.zeros_like(rows))
    halves = []
    for full, own in ((for_square, squares), (for_cross, crosses)):
        high, mid, low = pieces(full)
        tall = [high, high, mid, mid, low, high, own, own, own, jnp.zeros_like(own)]
        tall += [jnp.zeros_like(own)] * 6
        halves.append(jnp.concatenate(tall, axis=0).T)
    return jnp.concatenate(halves, axis=0).astype(BF16)


def local_setup(pos_ref, dir_ref, rows_ref, feature_ref, left_ref, center_ref):
    row = lax.broadcasted_iota(jnp.int32, (8, LANES), 0)
    for block in range(pos_ref.shape[1] // LANES):
        span = slice(block * LANES, (block + 1) * LANES)
        rows = jnp.concatenate(
            [pos_ref[:, span], dir_ref[:, span], jnp.zeros((2, LANES), F32)], axis=0
        )
        center = jnp.mean(rows, axis=1, keepdims=True)
        rows = rows - center
        center_ref[block] = jnp.broadcast_to(center, (8, LANES))
        rows_ref[block] = rows
        feature_ref[block] = local_operands(rows)
        left_ref[block] = remote_operands(rows)[1]


def split(value):
    high = value.astype(BF16)
    return high, (value - high.astype(F32)).astype(BF16)


def pair_coefficients(product):
    squared = jnp.minimum(product[:LANES], 1.0)
    along = product[LANES:]
    log_twice = TWICE_LN2 * lax.log2(squared)
    excess = squared - 1.0
    ratio = excess / squared
    return (
        split(excess * (log_twice + ratio)),
        split((log_twice + ratio * (4.0 - ratio)) * along),
    )


def pair_sums(grad, curv, left, right, remote):
    by_local = jnp.concatenate(
        [jnp.concatenate([grad[k], curv[k]], axis=1) for k in range(2)], axis=0
    )
    by_remote = jnp.concatenate(
        [jnp.concatenate([grad[k].T, curv[k].T], axis=1) for k in range(2)], axis=0
    )
    for_remote = lax.dot_general(twice_wide(left), by_local, NN, preferred_element_type=F32)
    for_local = lax.dot_general(twice_wide(right), by_remote, NN, preferred_element_type=F32)
    return own_terms(remote, fold(for_remote)), fold(for_local)


def eight_rows(six):
    return jnp.concatenate([six, jnp.zeros((2, LANES), F32)], axis=0)


def cross_kernel(
    local_ref, face_ref, pos_ref, dir_ref, incoming_ref,
    sums_ref, back_ref, rows_ref, feature_ref, left_ref, center_ref,
):
    local_setup(pos_ref, dir_ref, rows_ref, feature_ref, left_ref, center_ref)
    sums_ref[...] = jnp.zeros_like(sums_ref)
    back_ref[...] = jnp.zeros_like(back_ref)

    def some(step, carry):
        pairs = [step * 4 + k for k in range(4)]
        blocks = [local_ref[pair] for pair in pairs]
        rows = [pl.ds(face_ref[pair] * SIX, SIX) for pair in pairs]
        remotes = [
            eight_rows(incoming_ref[row, :]) - center_ref[block] for block, row in zip(blocks, rows)
        ]
        operands = [remote_operands(remote) for remote in remotes]
        products = [
            lax.dot_general(
                feature_ref[block, :, : right.shape[0]], right, NN, preferred_element_type=F32
            )
            for block, (right, _) in zip(blocks, operands)
        ]
        for block, row, remote, (_, right), product in zip(
            blocks, rows, remotes, operands, products
        ):
            grad, curv = pair_coefficients(product)
            remote, local = pair_sums(grad, curv, left_ref[block], right, remote)
            back_ref[row, :] += remote[:SIX]
            sums_ref[block] += local
        return carry

    count = jnp.where(lax.axis_index("body") > 0, local_ref.shape[0] // 4, 0)
    lax.fori_loop(0, count, some, 0)


def main_kernel(
    plan_ref, arrived_ref, back_ref, sums_in_ref, rows_ref, feature_ref, left_ref, center_ref,
    return_ref, terms_ref,
    sums_ref, list_ref, table_ref, sem,
    *buffers,
):
    peers = arrived_ref.shape[0] // MSG
    slots = 2 * peers
    num_blocks = terms_ref.shape[0]
    marks = arrived_ref[pl.ds(RET, peers, stride=MSG), :].astype(BF16)
    pick = (
        lax.broadcasted_iota(jnp.int32, (16, LANES), 0)
        == lax.broadcasted_iota(jnp.int32, (16, LANES), 1)
    ).astype(BF16)
    found = lax.dot_general(pick, marks, NT, preferred_element_type=F32)
    wide = jnp.concatenate([found[0:1], found[1:2]], axis=1)
    valid = wide >= 0.0
    slot = lax.broadcasted_iota(jnp.int32, (1, slots), 1)
    one = lax.broadcasted_iota(jnp.int32, (slots, slots), 0)
    before = (one < lax.broadcasted_iota(jnp.int32, (slots, slots), 1)).astype(BF16)
    ones = jnp.broadcast_to(valid.astype(F32), (16, slots)).astype(BF16)
    place = lax.dot_general(ones, before, NN, preferred_element_type=F32)[0:1]
    hot = (one.astype(F32) == place) & valid
    row = lax.broadcasted_iota(jnp.int32, (16, slots), 0)
    second = slot >= peers
    peer = jnp.where(second, slot - peers, slot).astype(F32)
    codes = jnp.where(row == 0, jnp.broadcast_to(wide, (16, slots)), 0.0)
    codes = jnp.where(row == 1, jnp.broadcast_to(peer, (16, slots)), codes)
    codes = jnp.where(row == 2, jnp.broadcast_to(second.astype(F32), (16, slots)), codes)
    ordered = lax.dot_general(
        codes.astype(BF16), hot.astype(F32).astype(BF16), NT, preferred_element_type=F32
    )
    ordered = ordered[:8].astype(jnp.int32)
    total = jnp.sum(valid.astype(F32), axis=1, keepdims=True).astype(jnp.int32)
    row = row[:8]
    base = ordered[1:2]
    shift = ordered[2:3] * SIX
    table = jnp.where(row == 0, ordered[0:1], 0)
    table = jnp.where(row == 1, base * MSG + shift, table)
    table = jnp.where(row == 2, base * RET + shift, table)
    list_ref[:, :slots] = jnp.where(row == 3, total, table)
    copy = pltpu.make_async_copy(list_ref, table_ref, sem)
    copy.start()
    sums_ref[0:num_blocks] = sums_in_ref[...]
    sums_ref[num_blocks] = jnp.zeros((8, 2 * LANES), F32)
    copy.wait()
    count = table_ref[3, 0]

    def listed(group, k):
        return jnp.clip(group * GROUP + k, 0, count - 1)

    def distances(group, dist_ref, right_ref, remote_ref):
        for k in range(GROUP):
            pair = listed(group, k)
            block = table_ref[0, pair]
            rows = eight_rows(arrived_ref[pl.ds(table_ref[1, pair], SIX), :]) - center_ref[block]
            right, sums_right = remote_operands(rows)
            remote_ref[k] = rows
            right_ref[k] = sums_right
            dist_ref[k] = lax.dot_general(
                feature_ref[block, :, : right.shape[0]], right, NN, preferred_element_type=F32
            )

    def sums(group, dist_ref, right_ref, remote_ref):
        for k in range(GROUP):
            pair = group * GROUP + k
            known = listed(group, k)
            block = table_ref[0, known]
            target = jnp.where(pair < count, block, num_blocks)
            grad, curv = pair_coefficients(dist_ref[k])
            remote, local = pair_sums(grad, curv, left_ref[block], right_ref[k], remote_ref[k])
            return_ref[pl.ds(table_ref[2, known], SIX), :] = remote[:SIX]
            sums_ref[target] += local

    sets = [buffers[k::IN_TURN] for k in range(IN_TURN)]

    def some_groups(step, carry):
        group = IN_TURN * step
        for k in range(1, IN_TURN):
            distances(group + k, *sets[k])
            sums(group + k - 1, *sets[k - 1])
        distances(group + IN_TURN, *sets[0])
        sums(group + IN_TURN - 1, *sets[-1])
        return carry

    @pl.when(count > 0)
    def _():
        distances(0, *sets[0])
        lax.fori_loop(
            0, (count + IN_TURN * GROUP - 1) // (IN_TURN * GROUP), some_groups, 0
        )

    for block in range(num_blocks):
        terms_ref[block] = own_terms(rows_ref[block], sums_ref[block])
    faces = back_ref.shape[0] // SIX
    for face in range(faces):
        block = plan_ref[plan_ref.shape[0] - faces + face]
        terms_ref[block, 0:SIX, :] += back_ref[face * SIX : face * SIX + SIX, :]


def finish_kernel(
    num_pairs, plan_ref, returned_ref, terms_ref,
    grad_ref, hess_ref,
    total_ref,
):
    num_blocks = terms_ref.shape[0]
    pairs = num_pairs
    total_ref[0:num_blocks] = terms_ref[...]
    count = plan_ref[2 * pairs]

    def some(step, carry):
        for k in range(UNROLL):
            pair = step * UNROLL + k
            block = jnp.where(pair < count, plan_ref[pairs + pair], num_blocks)
            total_ref[block, 0:SIX, :] += returned_ref[pl.ds(plan_ref[pair], SIX), :]
        return carry

    lax.fori_loop(0, (count + UNROLL - 1) // UNROLL, some, 0)
    for block in range(num_blocks):
        span = slice(block * LANES, (block + 1) * LANES)
        grad_ref[:, span] = SCALE * total_ref[block, 0:3, :]
        hess_ref[:, span] = SCALE * total_ref[block, 3:6, :]


def smem():
    return pl.BlockSpec(memory_space=pltpu.SMEM)


def vmem():
    return pl.BlockSpec(memory_space=pltpu.VMEM)


def limit(mib):
    return pltpu.CompilerParams(vmem_limit_bytes=mib << 20)


def on_chip(*shape, dtype=F32):
    return pltpu.VMEM(shape, dtype)


def held(*values):
    return [pltpu.with_memory_space_constraint(value, pltpu.VMEM) for value in values]


def exchange(rows, peers):
    count = rows.shape[0] // peers
    return lax.all_to_all(
        rows.reshape(peers, count, 1, LANES), "blk", split_axis=0, concat_axis=0, tiled=True
    ).reshape(rows.shape)


def per_device(
    positions, direction, pair_local, pair_peer, pair_shift, pair_count,
    face_index, cross_local, cross_face,
):
    num_blocks = positions.shape[1] // LANES
    peers = lax.axis_size("blk")
    faces = face_index.shape[0]
    setup = (
        on_chip(num_blocks, 8, LANES),
        on_chip(num_blocks, 2 * LANES, LANES, dtype=BF16),
        on_chip(num_blocks, 32, LANES, dtype=BF16),
        on_chip(num_blocks, 8, LANES),
    )
    send, face_rows, plan = pl.pallas_call(
        pack_kernel,
        name="pack",
        out_shape=(
            on_chip(peers * MSG, LANES),
            on_chip(faces * SIX, LANES),
            pltpu.SMEM((2 * pair_local.shape[0] + 1 + faces,), jnp.int32),
        ),
        in_specs=[smem()] * 5 + [vmem()] * 2,
        out_specs=(vmem(), vmem(), smem()),
        scratch_shapes=[pltpu.SMEM((peers,), jnp.int32)],
    )(pair_local, pair_peer, pair_shift, pair_count, face_index, positions, direction)
    arrived = exchange(send, peers)
    incoming = from_behind(face_rows, "body", 1)
    sums, back, *local = pl.pallas_call(
        cross_kernel,
        name="cross",
        compiler_params=limit(8),
        out_shape=(on_chip(num_blocks, 8, 2 * LANES), on_chip(faces * SIX, LANES)) + setup,
        in_specs=[smem()] * 2 + [vmem()] * 3,
        out_specs=(vmem(),) * 6,
    )(cross_local, cross_face, positions, direction, *held(incoming))
    face_back = from_behind(back, "body", -1)
    outgoing, terms = pl.pallas_call(
        main_kernel,
        name="pairs",
        compiler_params=limit(8),
        out_shape=(on_chip(peers * RET, LANES), on_chip(num_blocks, 8, LANES)),
        in_specs=[smem()] + [vmem()] * 7,
        out_specs=(vmem(), vmem()),
        scratch_shapes=[
            pltpu.VMEM((num_blocks + 1, 8, 2 * LANES), F32),
            pltpu.VMEM((8, LANES), jnp.int32),
            pltpu.SMEM((8, LANES), jnp.int32),
            pltpu.SemaphoreType.DMA,
        ]
        + [pltpu.VMEM((GROUP, 2 * LANES, LANES), F32)] * IN_TURN
        + [pltpu.VMEM((GROUP, 32, LANES), BF16)] * IN_TURN
        + [pltpu.VMEM((GROUP, 8, LANES), F32)] * IN_TURN,
    )(plan, *held(arrived, face_back, sums, *local))
    returned = exchange(outgoing, peers)
    return pl.pallas_call(
        functools.partial(finish_kernel, pair_local.shape[0]),
        name="finish",
        out_shape=[jax.ShapeDtypeStruct((3, num_blocks * LANES), F32)] * 2,
        in_specs=[smem()] + [vmem()] * 2,
        out_specs=(vmem(), vmem()),
        scratch_shapes=[pltpu.VMEM((num_blocks + 1, 8, LANES), F32)],
    )(plan, *held(returned, terms))


def solution(mesh):
    split_all = P(("blk", "body"))
    wide = P(None, ("blk", "body"))
    return jax.shard_map(
        per_device,
        mesh=mesh,
        in_specs=(wide, wide) + (split_all,) * 7,
        out_specs=(wide, wide),
        check_vma=False,
    )
```

```python
import jax
import jax.numpy as jnp
from jax import lax
from jax.experimental import pallas as pl
from jax.experimental.pallas import tpu as pltpu
from jax.sharding import PartitionSpec as P

XI = 0.1
TWICE_LN2 = 1.3862943611198906
SCALE = 0.02
LANES = 128
SIX = 6
MSG = 13
RET = 12
GROUP = 3
IN_TURN = 3
UNROLL = 4
F32 = jnp.float32
BF16 = jnp.bfloat16
NN = (((1,), (0,)), ((), ()))
NT = (((1,), (1,)), ((), ()))


def from_behind(value, axis, steps):
    count = lax.axis_size(axis)
    first, last = (max(0, -steps), min(count, count - steps))
    return lax.ppermute(value, axis, [(source, source + steps) for source in range(first, last)])


def put_block(target_ref, start, pos_ref, dir_ref, block):
    cols = pl.ds(pl.multiple_of(block * LANES, LANES), LANES)
    target_ref[pl.ds(start, 3), :] = pos_ref[:, cols]
    target_ref[pl.ds(start + 3, 3), :] = dir_ref[:, cols]


def pack_kernel(
    local_ref, peer_ref, shift_ref, count_ref, face_ref, pos_ref, dir_ref,
    send_ref, faces_ref, plan_ref, used_ref,
):
    peers = used_ref.shape[0]
    pairs = local_ref.shape[0]
    num_blocks = pos_ref.shape[1] // LANES
    count = count_ref[0]
    lane = lax.broadcasted_iota(jnp.int32, (1, LANES), 1)
    unused = jnp.full((1, LANES), -1.0, F32)
    for peer in range(peers):
        used_ref[peer] = 0
        row = peer * MSG + RET
        send_ref[row : row + 1, :] = unused

    def some(step, carry):
        for k in range(UNROLL):
            pair = step * UNROLL + k
            near = local_ref[pair]
            peer = peer_ref[pair]
            far = lax.rem(near + shift_ref[pair], num_blocks)
            mark = jnp.where(pair < count, far, -1).astype(F32)
            rank = used_ref[peer]
            used_ref[peer] = rank + 1
            plan_ref[pair] = peer * RET + rank * SIX
            plan_ref[pairs + pair] = near
            put_block(send_ref, peer * MSG + rank * SIX, pos_ref, dir_ref, near)
            pltpu.store(
                send_ref.at[pl.ds(peer * MSG + RET, 1), :],
                jnp.broadcast_to(mark, (1, LANES)),
                mask=lane == rank,
            )
        return carry

    lax.fori_loop(0, (count + UNROLL - 1) // UNROLL, some, 0)
    plan_ref[2 * pairs] = count
    for face in range(face_ref.shape[0]):
        block = face_ref[face]
        plan_ref[2 * pairs + 1 + face] = block
        put_block(faces_ref, face * SIX, pos_ref, dir_ref, block)


def pieces(value):
    high = value.astype(BF16).astype(F32)
    rest = value - high
    mid = rest.astype(BF16).astype(F32)
    return high, mid, rest - mid


def own_terms(rows, sums):
    row = lax.broadcasted_iota(jnp.int32, (8, LANES), 0)
    by_grad = sums[:, :LANES]
    by_curv = sums[:, LANES:]
    first = rows * by_grad[6:7, :] - by_grad
    second = rows * by_curv[6:7, :] - by_curv
    shifted = pltpu.roll(second, 3, 0)
    return first + jnp.where((row >= 3) & (row < 6), shifted, 0.0)


def fold(product):
    return product[0:8] + product[8:16] + product[16:24]


def twice_wide(tall):
    return jnp.concatenate([tall, tall], axis=1)


def remote_operands(rows):
    row = lax.broadcasted_iota(jnp.int32, (8, LANES), 0)
    twice = jnp.where(row == 6, -2.0, -2.0 * rows)
    high, mid, low = pieces(twice)
    products = twice * jnp.where(row < 3, twice, pltpu.roll(twice, 3, 0))
    p_high, p_mid, p_low = pieces(products)
    zero = jnp.zeros_like(low)
    high_mid = jnp.concatenate([high, mid], axis=0).astype(BF16)
    high_low = jnp.concatenate([high, low], axis=0).astype(BF16)
    low_zero = jnp.concatenate([low, zero], axis=0).astype(BF16)
    p_high_mid = jnp.concatenate([p_high, p_mid], axis=0).astype(BF16)
    p_low_zero = jnp.concatenate([p_low, zero], axis=0).astype(BF16)
    distances = jnp.concatenate([high_mid, high_mid, high_low, p_high_mid, p_low_zero], axis=0)
    return distances, jnp.concatenate([high_mid, low_zero], axis=0)


def local_operands(rows):
    row = lax.broadcasted_iota(jnp.int32, (8, LANES), 0)
    square = jnp.sum(rows[0:3] * rows[0:3], axis=0, keepdims=True) + XI
    cross = jnp.sum(rows[0:3] * rows[3:6], axis=0, keepdims=True)
    for_square = jnp.where(row < 3, rows, jnp.where(row == 6, -0.5 * square, 0.0))
    swapped = jnp.where(row < 3, pltpu.roll(rows, 5, 0), pltpu.roll(rows, 3, 0))
    for_cross = jnp.where(row < 6, swapped, jnp.where(row == 6, -cross, 0.0))
    squares = jnp.where(row < 3, 0.25, jnp.zeros_like(rows))
    crosses = jnp.where((row >= 3) & (row < 6), 0.5, jnp.zeros_like(rows))
    halves = []
    for full, own in ((for_square, squares), (for_cross, crosses)):
        high, mid, low = pieces(full)
        tall = [high, high, mid, mid, low, high, own, own, own, jnp.zeros_like(own)]
        tall += [jnp.zeros_like(own)] * 6
        halves.append(jnp.concatenate(tall, axis=0).T)
    return jnp.concatenate(halves, axis=0).astype(BF16)


def local_setup(pos_ref, dir_ref, rows_ref, feature_ref, left_ref, center_ref):
    row = lax.broadcasted_iota(jnp.int32, (8, LANES), 0)
    for block in range(pos_ref.shape[1] // LANES):
        span = slice(block * LANES, (block + 1) * LANES)
        rows = jnp.concatenate(
            [pos_ref[:, span], dir_ref[:, span], jnp.zeros((2, LANES), F32)], axis=0
        )
        center = jnp.mean(rows, axis=1, keepdims=True)
        rows = rows - center
        center_ref[block] = jnp.broadcast_to(center, (8, LANES))
        rows_ref[block] = rows
        feature_ref[block] = local_operands(rows)
        left_ref[block] = remote_operands(rows)[1]


def split(value):
    high = value.astype(BF16)
    return high, (value - high.astype(F32)).astype(BF16)


def pair_coefficients(product):
    squared = jnp.minimum(product[:LANES], 1.0)
    along = product[LANES:]
    log_twice = TWICE_LN2 * lax.log2(squared)
    excess = squared - 1.0
    ratio = excess / squared
    return (
        split(excess * (log_twice + ratio)),
        split((log_twice + ratio * (4.0 - ratio)) * along),
    )


def pair_sums(grad, curv, left, right, remote):
    by_local = jnp.concatenate(
        [jnp.concatenate([grad[k], curv[k]], axis=1) for k in range(2)], axis=0
    )
    by_remote = jnp.concatenate(
        [jnp.concatenate([grad[k].T, curv[k].T], axis=1) for k in range(2)], axis=0
    )
    for_remote = lax.dot_general(twice_wide(left), by_local, NN, preferred_element_type=F32)
    for_local = lax.dot_general(twice_wide(right), by_remote, NN, preferred_element_type=F32)
    return own_terms(remote, fold(for_remote)), fold(for_local)


def eight_rows(six):
    return jnp.concatenate([six, jnp.zeros((2, LANES), F32)], axis=0)


def cross_kernel(
    local_ref, face_ref, pos_ref, dir_ref, incoming_ref,
    sums_ref, back_ref, rows_ref, feature_ref, left_ref, center_ref,
):
    local_setup(pos_ref, dir_ref, rows_ref, feature_ref, left_ref, center_ref)
    sums_ref[...] = jnp.zeros_like(sums_ref)
    back_ref[...] = jnp.zeros_like(back_ref)

    def some(step, carry):
        pairs = [step * 4 + k for k in range(4)]
        blocks = [local_ref[pair] for pair in pairs]
        rows = [pl.ds(face_ref[pair] * SIX, SIX) for pair in pairs]
        remotes = [
            eight_rows(incoming_ref[row, :]) - center_ref[block] for block, row in zip(blocks, rows)
        ]
        operands = [remote_operands(remote) for remote in remotes]
        products = [
            lax.dot_general(
                feature_ref[block, :, : right.shape[0]], right, NN, preferred_element_type=F32
            )
            for block, (right, _) in zip(blocks, operands)
        ]
        for block, row, remote, (_, right), product in zip(
            blocks, rows, remotes, operands, products
        ):
            grad, curv = pair_coefficients(product)
            remote, local = pair_sums(grad, curv, left_ref[block], right, remote)
            back_ref[row, :] += remote[:SIX]
            sums_ref[block] += local
        return carry

    count = jnp.where(lax.axis_index("body") > 0, local_ref.shape[0] // 4, 0)
    lax.fori_loop(0, count, some, 0)


def main_kernel(
    arrived_ref, sums_in_ref, rows_ref, feature_ref, left_ref, center_ref,
    return_ref, terms_ref,
    sums_ref, list_ref, table_ref, sem,
    *buffers,
):
    peers = arrived_ref.shape[0] // MSG
    slots = 2 * peers
    num_blocks = terms_ref.shape[0]
    marks = arrived_ref[pl.ds(RET, peers, stride=MSG), :].astype(BF16)
    pick = (
        lax.broadcasted_iota(jnp.int32, (16, LANES), 0)
        == lax.broadcasted_iota(jnp.int32, (16, LANES), 1)
    ).astype(BF16)
    found = lax.dot_general(pick, marks, NT, preferred_element_type=F32)
    wide = jnp.concatenate([found[0:1], found[1:2]], axis=1)
    valid = wide >= 0.0
    slot = lax.broadcasted_iota(jnp.int32, (1, slots), 1)
    one = lax.broadcasted_iota(jnp.int32, (slots, slots), 0)
    before = (one < lax.broadcasted_iota(jnp.int32, (slots, slots), 1)).astype(BF16)
    ones = jnp.broadcast_to(valid.astype(F32), (16, slots)).astype(BF16)
    place = lax.dot_general(ones, before, NN, preferred_element_type=F32)[0:1]
    hot = (one.astype(F32) == place) & valid
    row = lax.broadcasted_iota(jnp.int32, (16, slots), 0)
    second = slot >= peers
    peer = jnp.where(second, slot - peers, slot).astype(F32)
    codes = jnp.where(row == 0, jnp.broadcast_to(wide, (16, slots)), 0.0)
    codes = jnp.where(row == 1, jnp.broadcast_to(peer, (16, slots)), codes)
    codes = jnp.where(row == 2, jnp.broadcast_to(second.astype(F32), (16, slots)), codes)
    ordered = lax.dot_general(
        codes.astype(BF16), hot.astype(F32).astype(BF16), NT, preferred_element_type=F32
    )
    ordered = ordered[:8].astype(jnp.int32)
    total = jnp.sum(valid.astype(F32), axis=1, keepdims=True).astype(jnp.int32)
    row = row[:8]
    base = ordered[1:2]
    shift = ordered[2:3] * SIX
    table = jnp.where(row == 0, ordered[0:1], 0)
    table = jnp.where(row == 1, base * MSG + shift, table)
    table = jnp.where(row == 2, base * RET + shift, table)
    list_ref[:, :slots] = jnp.where(row == 3, total, table)
    copy = pltpu.make_async_copy(list_ref, table_ref, sem)
    copy.start()
    sums_ref[0:num_blocks] = sums_in_ref[...]
    sums_ref[num_blocks] = jnp.zeros((8, 2 * LANES), F32)
    copy.wait()
    count = table_ref[3, 0]

    def listed(group, k):
        return jnp.clip(group * GROUP + k, 0, count - 1)

    def distances(group, dist_ref, right_ref, remote_ref):
        for k in range(GROUP):
            pair = listed(group, k)
            block = table_ref[0, pair]
            rows = eight_rows(arrived_ref[pl.ds(table_ref[1, pair], SIX), :]) - center_ref[block]
            right, sums_right = remote_operands(rows)
            remote_ref[k] = rows
            right_ref[k] = sums_right
            dist_ref[k] = lax.dot_general(
                feature_ref[block, :, : right.shape[0]], right, NN, preferred_element_type=F32
            )

    def sums(group, dist_ref, right_ref, remote_ref):
        for k in range(GROUP):
            pair = group * GROUP + k
            known = listed(group, k)
            block = table_ref[0, known]
            target = jnp.where(pair < count, block, num_blocks)
            grad, curv = pair_coefficients(dist_ref[k])
            remote, local = pair_sums(grad, curv, left_ref[block], right_ref[k], remote_ref[k])
            return_ref[pl.ds(table_ref[2, known], SIX), :] = remote[:SIX]
            sums_ref[target] += local

    sets = [buffers[k::IN_TURN] for k in range(IN_TURN)]

    def some_groups(step, carry):
        group = IN_TURN * step
        for k in range(1, IN_TURN):
            distances(group + k, *sets[k])
            sums(group + k - 1, *sets[k - 1])
        distances(group + IN_TURN, *sets[0])
        sums(group + IN_TURN - 1, *sets[-1])
        return carry

    @pl.when(count > 0)
    def _():
        distances(0, *sets[0])
        lax.fori_loop(
            0, (count + IN_TURN * GROUP - 1) // (IN_TURN * GROUP), some_groups, 0
        )

    for block in range(num_blocks):
        terms_ref[block] = own_terms(rows_ref[block], sums_ref[block])


def finish_kernel(
    plan_ref, returned_ref, terms_ref, back_ref,
    grad_ref, hess_ref,
    total_ref,
):
    num_blocks = terms_ref.shape[0]
    faces = back_ref.shape[0] // SIX
    pairs = (plan_ref.shape[0] - 1 - faces) // 2
    total_ref[0:num_blocks] = terms_ref[...]
    for face in range(faces):
        block = plan_ref[2 * pairs + 1 + face]
        total_ref[block, 0:SIX, :] += back_ref[face * SIX : face * SIX + SIX, :]
    count = plan_ref[2 * pairs]

    def some(step, carry):
        for k in range(UNROLL):
            pair = step * UNROLL + k
            block = jnp.where(pair < count, plan_ref[pairs + pair], num_blocks)
            total_ref[block, 0:SIX, :] += returned_ref[pl.ds(plan_ref[pair], SIX), :]
        return carry

    lax.fori_loop(0, (count + UNROLL - 1) // UNROLL, some, 0)
    for block in range(num_blocks):
        span = slice(block * LANES, (block + 1) * LANES)
        grad_ref[:, span] = SCALE * total_ref[block, 0:3, :]
        hess_ref[:, span] = SCALE * total_ref[block, 3:6, :]


def smem():
    return pl.BlockSpec(memory_space=pltpu.SMEM)


def vmem():
    return pl.BlockSpec(memory_space=pltpu.VMEM)


def limit(mib):
    return pltpu.CompilerParams(vmem_limit_bytes=mib << 20)


def on_chip(*shape, dtype=F32):
    return pltpu.VMEM(shape, dtype)


def held(*values):
    return [pltpu.with_memory_space_constraint(value, pltpu.VMEM) for value in values]


def exchange(rows, peers):
    count = rows.shape[0] // peers
    return lax.all_to_all(
        rows.reshape(peers, count, 1, LANES), "blk", split_axis=0, concat_axis=0, tiled=True
    ).reshape(rows.shape)


def per_device(
    positions, direction, pair_local, pair_peer, pair_shift, pair_count,
    face_index, cross_local, cross_face,
):
    num_blocks = positions.shape[1] // LANES
    peers = lax.axis_size("blk")
    faces = face_index.shape[0]
    setup = (
        on_chip(num_blocks, 8, LANES),
        on_chip(num_blocks, 2 * LANES, LANES, dtype=BF16),
        on_chip(num_blocks, 32, LANES, dtype=BF16),
        on_chip(num_blocks, 8, LANES),
    )
    send, face_rows, plan = pl.pallas_call(
        pack_kernel,
        name="pack",
        out_shape=(
            on_chip(peers * MSG, LANES),
            on_chip(faces * SIX, LANES),
            pltpu.SMEM((2 * pair_local.shape[0] + 1 + faces,), jnp.int32),
        ),
        in_specs=[smem()] * 5 + [vmem()] * 2,
        out_specs=(vmem(), vmem(), smem()),
        scratch_shapes=[pltpu.SMEM((peers,), jnp.int32)],
    )(pair_local, pair_peer, pair_shift, pair_count, face_index, positions, direction)
    arrived = exchange(send, peers)
    incoming = from_behind(face_rows, "body", 1)
    sums, back, *local = pl.pallas_call(
        cross_kernel,
        name="cross",
        compiler_params=limit(8),
        out_shape=(on_chip(num_blocks, 8, 2 * LANES), on_chip(faces * SIX, LANES)) + setup,
        in_specs=[smem()] * 2 + [vmem()] * 3,
        out_specs=(vmem(),) * 6,
    )(cross_local, cross_face, positions, direction, *held(incoming))
    face_back = from_behind(back, "body", -1)
    outgoing, terms = pl.pallas_call(
        main_kernel,
        name="pairs",
        compiler_params=limit(8),
        out_shape=(on_chip(peers * RET, LANES), on_chip(num_blocks, 8, LANES)),
        in_specs=[vmem()] * 6,
        out_specs=(vmem(), vmem()),
        scratch_shapes=[
            pltpu.VMEM((num_blocks + 1, 8, 2 * LANES), F32),
            pltpu.VMEM((8, LANES), jnp.int32),
            pltpu.SMEM((8, LANES), jnp.int32),
            pltpu.SemaphoreType.DMA,
        ]
        + [pltpu.VMEM((GROUP, 2 * LANES, LANES), F32)] * IN_TURN
        + [pltpu.VMEM((GROUP, 32, LANES), BF16)] * IN_TURN
        + [pltpu.VMEM((GROUP, 8, LANES), F32)] * IN_TURN,
    )(*held(arrived, sums, *local))
    returned = exchange(outgoing, peers)
    return pl.pallas_call(
        finish_kernel,
        name="finish",
        out_shape=[jax.ShapeDtypeStruct((3, num_blocks * LANES), F32)] * 2,
        in_specs=[smem()] + [vmem()] * 3,
        out_specs=(vmem(), vmem()),
        scratch_shapes=[pltpu.VMEM((num_blocks + 1, 8, LANES), F32)],
    )(plan, *held(returned, terms, face_back))


def solution(mesh):
    split_all = P(("blk", "body"))
    wide = P(None, ("blk", "body"))
    return jax.shard_map(
        per_device,
        mesh=mesh,
        in_specs=(wide, wide) + (split_all,) * 7,
        out_specs=(wide, wide),
        check_vma=False,
    )
```

```python
import jax
import jax.numpy as jnp
from jax import lax
from jax.experimental import pallas as pl
from jax.experimental.pallas import tpu as pltpu
from jax.sharding import PartitionSpec as P


XI = 0.1
TWICE_LN2 = 1.3862943611198906
SCALE = 0.02
LANES = 128
FACES = 4
SIX = 6
MSG = 13
RET = 12
GROUP = 3
IN_TURN = 3
UNROLL = 4
F32 = jnp.float32
BF16 = jnp.bfloat16
NN = (((1,), (0,)), ((), ()))
NT = (((1,), (1,)), ((), ()))


def from_behind(value, axis, steps):
    count = lax.axis_size(axis)
    first, last = (max(0, -steps), min(count, count - steps))
    return lax.ppermute(value, axis, [(source, source + steps) for source in range(first, last)])


def pack_kernel(
    local_ref, peer_ref, shift_ref, count_ref, face_ref, pos_ref, dir_ref,
    send_ref, faces_ref, plan_ref, used_ref, block_ref,
):
    peers = used_ref.shape[0]
    pairs = local_ref.shape[0]
    num_blocks = pos_ref.shape[1] // LANES
    count = count_ref[0]
    lane = lax.broadcasted_iota(jnp.int32, (1, LANES), 1)
    unused = jnp.full((1, LANES), -1.0, F32)
    for block in range(num_blocks):
        span = slice(block * LANES, (block + 1) * LANES)
        block_ref[block, 0:3, :] = pos_ref[:, span]
        block_ref[block, 3:6, :] = dir_ref[:, span]
    for peer in range(peers):
        used_ref[peer] = 0
        row = peer * MSG + RET
        send_ref[row : row + 1, :] = unused

    def some(step, carry):
        for k in range(UNROLL):
            pair = step * UNROLL + k
            near = local_ref[pair]
            peer = peer_ref[pair]
            far = jnp.bitwise_and(near + shift_ref[pair], num_blocks - 1)
            mark = jnp.where(pair < count, far, -1).astype(F32)
            rank = used_ref[peer]
            used_ref[peer] = rank + 1
            row = peer * RET + rank * SIX
            plan_ref[pair] = row
            plan_ref[pairs + pair] = near
            send_ref[pl.ds(row + peer, SIX), :] = block_ref[near, 0:SIX, :]
            pltpu.store(
                send_ref.at[pl.ds(peer * MSG + RET, 1), :],
                jnp.broadcast_to(mark, (1, LANES)),
                mask=lane == rank,
            )
        return carry

    lax.fori_loop(0, (count + UNROLL - 1) // UNROLL, some, 0)
    plan_ref[2 * pairs] = count
    for face in range(face_ref.shape[0]):
        block = face_ref[face]
        plan_ref[2 * pairs + 1 + face] = block
        faces_ref[face * SIX : face * SIX + SIX, :] = block_ref[block, 0:SIX, :]


def pieces(value):
    high = value.astype(BF16).astype(F32)
    rest = value - high
    mid = rest.astype(BF16).astype(F32)
    return high, mid, rest - mid


def own_terms(rows, sums):
    row = lax.broadcasted_iota(jnp.int32, (8, LANES), 0)
    by_grad = sums[:, :LANES]
    by_curv = sums[:, LANES:]
    first = rows * by_grad[6:7, :] - by_grad
    second = rows * by_curv[6:7, :] - by_curv
    shifted = pltpu.roll(second, 3, 0)
    return first + jnp.where((row >= 3) & (row < 6), shifted, 0.0)


def fold(product):
    return product[0:8] + product[8:16] + product[16:24]


def twice_wide(tall):
    return jnp.concatenate([tall, tall], axis=1)


def remote_operands(rows):
    row = lax.broadcasted_iota(jnp.int32, (8, LANES), 0)
    twice = jnp.where(row == 6, -2.0, -2.0 * rows)
    high, mid, low = pieces(twice)
    products = twice * jnp.where(row < 3, twice, pltpu.roll(twice, 3, 0))
    p_high, p_mid, p_low = pieces(products)
    zero = jnp.zeros_like(low)
    high_mid = jnp.concatenate([high, mid], axis=0).astype(BF16)
    high_low = jnp.concatenate([high, low], axis=0).astype(BF16)
    low_zero = jnp.concatenate([low, zero], axis=0).astype(BF16)
    p_high_mid = jnp.concatenate([p_high, p_mid], axis=0).astype(BF16)
    p_low_zero = jnp.concatenate([p_low, zero], axis=0).astype(BF16)
    distances = jnp.concatenate([high_mid, high_mid, high_low, p_high_mid, p_low_zero], axis=0)
    return distances, jnp.concatenate([high_mid, low_zero], axis=0)


def local_operands(rows):
    row = lax.broadcasted_iota(jnp.int32, (8, LANES), 0)
    square = jnp.sum(rows[0:3] * rows[0:3], axis=0, keepdims=True) + XI
    cross = jnp.sum(rows[0:3] * rows[3:6], axis=0, keepdims=True)
    for_square = jnp.where(row < 3, rows, jnp.where(row == 6, -0.5 * square, 0.0))
    swapped = jnp.where(row < 3, pltpu.roll(rows, 5, 0), pltpu.roll(rows, 3, 0))
    for_cross = jnp.where(row < 6, swapped, jnp.where(row == 6, -cross, 0.0))
    squares = jnp.where(row < 3, 0.25, jnp.zeros_like(rows))
    crosses = jnp.where((row >= 3) & (row < 6), 0.5, jnp.zeros_like(rows))
    halves = []
    for full, own in ((for_square, squares), (for_cross, crosses)):
        high, mid, low = pieces(full)
        tall = [high, high, mid, mid, low, high, own, own, own, jnp.zeros_like(own)]
        tall += [jnp.zeros_like(own)] * 6
        halves.append(jnp.concatenate(tall, axis=0).T)
    return jnp.concatenate(halves, axis=0).astype(BF16)


def local_setup(pos_ref, dir_ref, rows_ref, feature_ref, left_ref, center_ref):
    row = lax.broadcasted_iota(jnp.int32, (8, LANES), 0)
    for block in range(pos_ref.shape[1] // LANES):
        span = slice(block * LANES, (block + 1) * LANES)
        rows = jnp.concatenate(
            [pos_ref[:, span], dir_ref[:, span], jnp.zeros((2, LANES), F32)], axis=0
        )
        center = jnp.mean(rows, axis=1, keepdims=True)
        rows = rows - center
        center_ref[block] = jnp.broadcast_to(center, (8, LANES))
        rows_ref[block] = rows
        feature_ref[block] = local_operands(rows)
        left_ref[block] = remote_operands(rows)[1]


def split(value):
    high = value.astype(BF16)
    return high, (value - high.astype(F32)).astype(BF16)


def pair_coefficients(product):
    squared = jnp.minimum(product[:LANES], 1.0)
    along = product[LANES:]
    log_twice = TWICE_LN2 * lax.log2(squared)
    excess = squared - 1.0
    ratio = excess / squared
    return (
        split(excess * (log_twice + ratio)),
        split((log_twice + ratio * (4.0 - ratio)) * along),
    )


def pair_sums(grad, curv, left, right, remote):
    by_local = jnp.concatenate(
        [jnp.concatenate([grad[k], curv[k]], axis=1) for k in range(2)], axis=0
    )
    by_remote = jnp.concatenate(
        [jnp.concatenate([grad[k].T, curv[k].T], axis=1) for k in range(2)], axis=0
    )
    for_remote = lax.dot_general(twice_wide(left), by_local, NN, preferred_element_type=F32)
    for_local = lax.dot_general(twice_wide(right), by_remote, NN, preferred_element_type=F32)
    return own_terms(remote, fold(for_remote)), fold(for_local)


def eight_rows(six):
    return jnp.concatenate([six, jnp.zeros((2, LANES), F32)], axis=0)


def cross_kernel(
    local_ref, face_ref, pos_ref, dir_ref, incoming_ref,
    sums_ref, back_ref, rows_ref, feature_ref, left_ref, center_ref,
):
    local_setup(pos_ref, dir_ref, rows_ref, feature_ref, left_ref, center_ref)
    sums_ref[...] = jnp.zeros_like(sums_ref)
    back_ref[...] = jnp.zeros_like(back_ref)

    def some(step, carry):
        pairs = [step * 4 + k for k in range(4)]
        blocks = [local_ref[pair] for pair in pairs]
        rows = [pl.ds(face_ref[pair] * SIX, SIX) for pair in pairs]
        remotes = [
            eight_rows(incoming_ref[row, :]) - center_ref[block] for block, row in zip(blocks, rows)
        ]
        operands = [remote_operands(remote) for remote in remotes]
        products = [
            lax.dot_general(
                feature_ref[block, :, : right.shape[0]], right, NN, preferred_element_type=F32
            )
            for block, (right, _) in zip(blocks, operands)
        ]
        for block, row, remote, (_, right), product in zip(
            blocks, rows, remotes, operands, products
        ):
            grad, curv = pair_coefficients(product)
            remote, local = pair_sums(grad, curv, left_ref[block], right, remote)
            back_ref[row, :] += remote[:SIX]
            sums_ref[block] += local
        return carry

    count = jnp.where(lax.axis_index("body") > 0, local_ref.shape[0] // 4, 0)
    lax.fori_loop(0, count, some, 0)


def main_kernel(
    arrived_ref, sums_in_ref, rows_ref, feature_ref, left_ref, center_ref,
    return_ref, terms_ref,
    sums_ref, list_ref, table_ref, sem,
    *buffers,
):
    peers = arrived_ref.shape[0] // MSG
    slots = 2 * peers
    num_blocks = terms_ref.shape[0]
    marks = arrived_ref[pl.ds(RET, peers, stride=MSG), :].astype(BF16)
    pick = (
        lax.broadcasted_iota(jnp.int32, (16, LANES), 0)
        == lax.broadcasted_iota(jnp.int32, (16, LANES), 1)
    ).astype(BF16)
    found = lax.dot_general(pick, marks, NT, preferred_element_type=F32)
    wide = jnp.concatenate([found[0:1], found[1:2]], axis=1)
    valid = wide >= 0.0
    slot = lax.broadcasted_iota(jnp.int32, (1, slots), 1)
    one = lax.broadcasted_iota(jnp.int32, (slots, slots), 0)
    before = (one < lax.broadcasted_iota(jnp.int32, (slots, slots), 1)).astype(BF16)
    ones = jnp.broadcast_to(valid.astype(F32), (16, slots)).astype(BF16)
    place = lax.dot_general(ones, before, NN, preferred_element_type=F32)[0:1]
    hot = (one.astype(F32) == place) & valid
    row = lax.broadcasted_iota(jnp.int32, (16, slots), 0)
    second = slot >= peers
    peer = jnp.where(second, slot - peers, slot).astype(F32)
    codes = jnp.where(row == 0, jnp.broadcast_to(wide, (16, slots)), 0.0)
    codes = jnp.where(row == 1, jnp.broadcast_to(peer, (16, slots)), codes)
    codes = jnp.where(row == 2, jnp.broadcast_to(second.astype(F32), (16, slots)), codes)
    ordered = lax.dot_general(
        codes.astype(BF16), hot.astype(F32).astype(BF16), NT, preferred_element_type=F32
    )
    ordered = ordered[:8].astype(jnp.int32)
    total = jnp.sum(valid.astype(F32), axis=1, keepdims=True).astype(jnp.int32)
    row = row[:8]
    base = ordered[1:2]
    shift = ordered[2:3] * SIX
    table = jnp.where(row == 0, ordered[0:1], 0)
    table = jnp.where(row == 1, base * MSG + shift, table)
    table = jnp.where(row == 2, base * RET + shift, table)
    list_ref[:, :slots] = jnp.where(row == 3, total, table)
    copy = pltpu.make_async_copy(list_ref, table_ref, sem)
    copy.start()
    sums_ref[0:num_blocks] = sums_in_ref[...]
    sums_ref[num_blocks] = jnp.zeros((8, 2 * LANES), F32)
    copy.wait()
    count = table_ref[3, 0]

    def listed(group, k):
        return jnp.clip(group * GROUP + k, 0, count - 1)

    def distances(group, dist_ref, right_ref, remote_ref):
        for k in range(GROUP):
            pair = listed(group, k)
            block = table_ref[0, pair]
            rows = eight_rows(arrived_ref[pl.ds(table_ref[1, pair], SIX), :]) - center_ref[block]
            right, sums_right = remote_operands(rows)
            remote_ref[k] = rows
            right_ref[k] = sums_right
            dist_ref[k] = lax.dot_general(
                feature_ref[block, :, : right.shape[0]], right, NN, preferred_element_type=F32
            )

    def sums(group, dist_ref, right_ref, remote_ref):
        for k in range(GROUP):
            pair = group * GROUP + k
            known = listed(group, k)
            block = table_ref[0, known]
            target = jnp.where(pair < count, block, num_blocks)
            grad, curv = pair_coefficients(dist_ref[k])
            remote, local = pair_sums(grad, curv, left_ref[block], right_ref[k], remote_ref[k])
            return_ref[pl.ds(table_ref[2, known], SIX), :] = remote[:SIX]
            sums_ref[target] += local

    sets = [buffers[k::IN_TURN] for k in range(IN_TURN)]

    def some_groups(step, carry):
        group = IN_TURN * step
        for k in range(1, IN_TURN):
            distances(group + k, *sets[k])
            sums(group + k - 1, *sets[k - 1])
        distances(group + IN_TURN, *sets[0])
        sums(group + IN_TURN - 1, *sets[-1])
        return carry

    @pl.when(count > 0)
    def _():
        distances(0, *sets[0])
        lax.fori_loop(
            0, (count + IN_TURN * GROUP - 1) // (IN_TURN * GROUP), some_groups, 0
        )

    for block in range(num_blocks):
        terms_ref[block] = own_terms(rows_ref[block], sums_ref[block])


def gather_kernel(plan_ref, returned_ref, terms_ref, total_ref):
    num_blocks = terms_ref.shape[0]
    pairs = (plan_ref.shape[0] - 1 - FACES) // 2
    total_ref[0:num_blocks] = terms_ref[...]
    count = plan_ref[2 * pairs]

    def some(step, carry):
        for k in range(UNROLL):
            pair = step * UNROLL + k
            block = jnp.where(pair < count, plan_ref[pairs + pair], num_blocks)
            total_ref[block, 0:SIX, :] += returned_ref[pl.ds(plan_ref[pair], SIX), :]
        return carry

    lax.fori_loop(0, (count + UNROLL - 1) // UNROLL, some, 0)


def finish_kernel(plan_ref, total_ref, back_ref, grad_ref, hess_ref, sum_ref):
    sum_ref[...] = total_ref[...]
    for face in range(FACES):
        block = plan_ref[plan_ref.shape[0] - FACES + face]
        sum_ref[block, 0:SIX, :] += back_ref[face * SIX : face * SIX + SIX, :]
    for block in range(sum_ref.shape[0] - 1):
        span = slice(block * LANES, (block + 1) * LANES)
        grad_ref[:, span] = SCALE * sum_ref[block, 0:3, :]
        hess_ref[:, span] = SCALE * sum_ref[block, 3:6, :]


def smem():
    return pl.BlockSpec(memory_space=pltpu.SMEM)


def vmem():
    return pl.BlockSpec(memory_space=pltpu.VMEM)


def limit(mib):
    return pltpu.CompilerParams(vmem_limit_bytes=mib << 20)


def on_chip(*shape, dtype=F32):
    return pltpu.VMEM(shape, dtype)


def held(*values):
    return [pltpu.with_memory_space_constraint(value, pltpu.VMEM) for value in values]


def exchange(rows, peers):
    count = rows.shape[0] // peers
    return lax.all_to_all(
        rows.reshape(peers, count, 1, LANES), "blk", split_axis=0, concat_axis=0, tiled=True
    ).reshape(rows.shape)


def per_device(
    positions, direction, pair_local, pair_peer, pair_shift, pair_count,
    face_index, cross_local, cross_face,
):
    num_blocks = positions.shape[1] // LANES
    peers = lax.axis_size("blk")
    faces = face_index.shape[0]
    setup = (
        on_chip(num_blocks, 8, LANES),
        on_chip(num_blocks, 2 * LANES, LANES, dtype=BF16),
        on_chip(num_blocks, 32, LANES, dtype=BF16),
        on_chip(num_blocks, 8, LANES),
    )
    send, face_rows, plan = pl.pallas_call(
        pack_kernel,
        name="pack",
        out_shape=(
            on_chip(peers * MSG, LANES),
            on_chip(faces * SIX, LANES),
            pltpu.SMEM((2 * pair_local.shape[0] + 1 + faces,), jnp.int32),
        ),
        in_specs=[smem()] * 5 + [vmem()] * 2,
        out_specs=(vmem(), vmem(), smem()),
        scratch_shapes=[
            pltpu.SMEM((peers,), jnp.int32),
            pltpu.VMEM((num_blocks, 8, LANES), F32),
        ],
    )(pair_local, pair_peer, pair_shift, pair_count, face_index, positions, direction)
    arrived = exchange(send, peers)
    incoming = from_behind(face_rows, "body", 1)
    sums, back, *local = pl.pallas_call(
        cross_kernel,
        name="cross",
        compiler_params=limit(8),
        out_shape=(on_chip(num_blocks, 8, 2 * LANES), on_chip(faces * SIX, LANES)) + setup,
        in_specs=[smem()] * 2 + [vmem()] * 3,
        out_specs=(vmem(),) * 6,
    )(cross_local, cross_face, positions, direction, *held(incoming))
    face_back = from_behind(back, "body", -1)
    outgoing, terms = pl.pallas_call(
        main_kernel,
        name="pairs",
        compiler_params=limit(8),
        out_shape=(on_chip(peers * RET, LANES), on_chip(num_blocks, 8, LANES)),
        in_specs=[vmem()] * 6,
        out_specs=(vmem(), vmem()),
        scratch_shapes=[
            pltpu.VMEM((num_blocks + 1, 8, 2 * LANES), F32),
            pltpu.VMEM((8, LANES), jnp.int32),
            pltpu.SMEM((8, LANES), jnp.int32),
            pltpu.SemaphoreType.DMA,
        ]
        + [pltpu.VMEM((GROUP, 2 * LANES, LANES), F32)] * IN_TURN
        + [pltpu.VMEM((GROUP, 32, LANES), BF16)] * IN_TURN
        + [pltpu.VMEM((GROUP, 8, LANES), F32)] * IN_TURN,
    )(*held(arrived, sums, *local))
    returned = exchange(outgoing, peers)
    total = pl.pallas_call(
        gather_kernel,
        name="gather",
        compiler_params=limit(8),
        out_shape=on_chip(num_blocks + 1, 8, LANES),
        in_specs=[smem()] + [vmem()] * 2,
        out_specs=vmem(),
    )(plan, *held(returned, terms))
    return pl.pallas_call(
        finish_kernel,
        name="finish",
        out_shape=[jax.ShapeDtypeStruct((3, num_blocks * LANES), F32)] * 2,
        in_specs=[smem()] + [vmem()] * 2,
        out_specs=(vmem(), vmem()),
        scratch_shapes=[pltpu.VMEM((num_blocks + 1, 8, LANES), F32)],
    )(plan, *held(total, face_back))


def solution(mesh):
    split_all = P(("blk", "body"))
    wide = P(None, ("blk", "body"))

    return jax.shard_map(
        per_device,
        mesh=mesh,
        in_specs=(wide, wide) + (split_all,) * 7,
        out_specs=(wide, wide),
        check_vma=False,
    )
```

```python
import jax
import jax.numpy as jnp
from jax import lax
from jax.experimental import pallas as pl
from jax.experimental.pallas import tpu as pltpu
from jax.sharding import PartitionSpec as P


XI = 0.1
TWICE_LN2 = 1.3862943611198906
SCALE = 0.02
LANES = 128
FACES = 4
SIX = 6
MSG = 13
RET = 12
GROUP = 3
IN_TURN = 3
UNROLL = 4
F32 = jnp.float32
BF16 = jnp.bfloat16
NN = (((1,), (0,)), ((), ()))
NT = (((1,), (1,)), ((), ()))


def from_behind(value, axis, steps):
    count = lax.axis_size(axis)
    first, last = (max(0, -steps), min(count, count - steps))
    return lax.ppermute(value, axis, [(source, source + steps) for source in range(first, last)])


def pack_kernel(
    local_ref, peer_ref, shift_ref, count_ref, face_ref, pos_ref, dir_ref,
    send_ref, faces_ref, plan_ref, used_ref, block_ref,
):
    peers = used_ref.shape[0]
    pairs = local_ref.shape[0]
    num_blocks = pos_ref.shape[1] // LANES
    count = count_ref[0]
    lane = lax.broadcasted_iota(jnp.int32, (1, LANES), 1)
    mine = lax.axis_index("blk")
    unused = jnp.zeros((1, LANES), F32)
    for block in range(num_blocks):
        span = slice(block * LANES, (block + 1) * LANES)
        block_ref[block, 0:3, :] = pos_ref[:, span]
        block_ref[block, 3:6, :] = dir_ref[:, span]
    for peer in range(peers):
        used_ref[peer] = 0
        row = peer * MSG + RET
        send_ref[row : row + 1, :] = unused

    def some(step, carry):
        for k in range(UNROLL):
            pair = step * UNROLL + k
            near = local_ref[pair]
            peer = peer_ref[pair]
            far = jnp.bitwise_and(near + shift_ref[pair], num_blocks - 1)
            mark = jnp.where(pair < count, far + 1, 0).astype(F32)
            rank = used_ref[peer]
            used_ref[peer] = rank + 1
            row = peer * RET + rank * SIX
            plan_ref[pair] = row
            plan_ref[pairs + pair] = near
            send_ref[pl.ds(row + peer, SIX), :] = block_ref[near, 0:SIX, :]
            pltpu.store(
                send_ref.at[pl.ds(peer * MSG + RET, 1), :],
                jnp.broadcast_to(mark, (1, LANES)),
                mask=lane == rank * peers + mine,
            )
        return carry

    lax.fori_loop(0, (count + UNROLL - 1) // UNROLL, some, 0)
    plan_ref[2 * pairs] = count
    for face in range(face_ref.shape[0]):
        block = face_ref[face]
        plan_ref[2 * pairs + 1 + face] = block
        faces_ref[face * SIX : face * SIX + SIX, :] = block_ref[block, 0:SIX, :]


def pieces(value):
    high = value.astype(BF16).astype(F32)
    rest = value - high
    mid = rest.astype(BF16).astype(F32)
    return high, mid, rest - mid


def own_terms(rows, sums):
    row = lax.broadcasted_iota(jnp.int32, (8, LANES), 0)
    by_grad = sums[:, :LANES]
    by_curv = sums[:, LANES:]
    first = rows * by_grad[6:7, :] - by_grad
    second = rows * by_curv[6:7, :] - by_curv
    shifted = pltpu.roll(second, 3, 0)
    return first + jnp.where((row >= 3) & (row < 6), shifted, 0.0)


def fold(product):
    return product[0:8] + product[8:16] + product[16:24]


def twice_wide(tall):
    return jnp.concatenate([tall, tall], axis=1)


def remote_operands(rows):
    row = lax.broadcasted_iota(jnp.int32, (8, LANES), 0)
    twice = jnp.where(row == 6, -2.0, -2.0 * rows)
    high, mid, low = pieces(twice)
    products = twice * jnp.where(row < 3, twice, pltpu.roll(twice, 3, 0))
    p_high, p_mid, p_low = pieces(products)
    zero = jnp.zeros_like(low)
    high_mid = jnp.concatenate([high, mid], axis=0).astype(BF16)
    high_low = jnp.concatenate([high, low], axis=0).astype(BF16)
    low_zero = jnp.concatenate([low, zero], axis=0).astype(BF16)
    p_high_mid = jnp.concatenate([p_high, p_mid], axis=0).astype(BF16)
    p_low_zero = jnp.concatenate([p_low, zero], axis=0).astype(BF16)
    distances = jnp.concatenate([high_mid, high_mid, high_low, p_high_mid, p_low_zero], axis=0)
    return distances, jnp.concatenate([high_mid, low_zero], axis=0)


def local_operands(rows):
    row = lax.broadcasted_iota(jnp.int32, (8, LANES), 0)
    square = jnp.sum(rows[0:3] * rows[0:3], axis=0, keepdims=True) + XI
    cross = jnp.sum(rows[0:3] * rows[3:6], axis=0, keepdims=True)
    for_square = jnp.where(row < 3, rows, jnp.where(row == 6, -0.5 * square, 0.0))
    swapped = jnp.where(row < 3, pltpu.roll(rows, 5, 0), pltpu.roll(rows, 3, 0))
    for_cross = jnp.where(row < 6, swapped, jnp.where(row == 6, -cross, 0.0))
    squares = jnp.where(row < 3, 0.25, jnp.zeros_like(rows))
    crosses = jnp.where((row >= 3) & (row < 6), 0.5, jnp.zeros_like(rows))
    halves = []
    for full, own in ((for_square, squares), (for_cross, crosses)):
        high, mid, low = pieces(full)
        tall = [high, high, mid, mid, low, high, own, own, own, jnp.zeros_like(own)]
        tall += [jnp.zeros_like(own)] * 6
        halves.append(jnp.concatenate(tall, axis=0).T)
    return jnp.concatenate(halves, axis=0).astype(BF16)


def local_setup(pos_ref, dir_ref, rows_ref, feature_ref, left_ref, center_ref):
    row = lax.broadcasted_iota(jnp.int32, (8, LANES), 0)
    for block in range(pos_ref.shape[1] // LANES):
        span = slice(block * LANES, (block + 1) * LANES)
        rows = jnp.concatenate(
            [pos_ref[:, span], dir_ref[:, span], jnp.zeros((2, LANES), F32)], axis=0
        )
        center = jnp.mean(rows, axis=1, keepdims=True)
        rows = rows - center
        center_ref[block] = jnp.broadcast_to(center, (8, LANES))
        rows_ref[block] = rows
        feature_ref[block] = local_operands(rows)
        left_ref[block] = remote_operands(rows)[1]


def split(value):
    high = value.astype(BF16)
    return high, (value - high.astype(F32)).astype(BF16)


def pair_coefficients(product):
    squared = jnp.minimum(product[:LANES], 1.0)
    along = product[LANES:]
    log_twice = TWICE_LN2 * lax.log2(squared)
    excess = squared - 1.0
    ratio = excess / squared
    return (
        split(excess * (log_twice + ratio)),
        split((log_twice + ratio * (4.0 - ratio)) * along),
    )


def pair_sums(grad, curv, left, right, remote):
    by_local = jnp.concatenate(
        [jnp.concatenate([grad[k], curv[k]], axis=1) for k in range(2)], axis=0
    )
    by_remote = jnp.concatenate(
        [jnp.concatenate([grad[k].T, curv[k].T], axis=1) for k in range(2)], axis=0
    )
    for_remote = lax.dot_general(twice_wide(left), by_local, NN, preferred_element_type=F32)
    for_local = lax.dot_general(twice_wide(right), by_remote, NN, preferred_element_type=F32)
    return own_terms(remote, fold(for_remote)), fold(for_local)


def eight_rows(six):
    return jnp.concatenate([six, jnp.zeros((2, LANES), F32)], axis=0)


def cross_kernel(
    local_ref, face_ref, pos_ref, dir_ref, incoming_ref,
    sums_ref, back_ref, rows_ref, feature_ref, left_ref, center_ref,
):
    local_setup(pos_ref, dir_ref, rows_ref, feature_ref, left_ref, center_ref)
    sums_ref[...] = jnp.zeros_like(sums_ref)
    back_ref[...] = jnp.zeros_like(back_ref)

    def some(step, carry):
        pairs = [step * 4 + k for k in range(4)]
        blocks = [local_ref[pair] for pair in pairs]
        rows = [pl.ds(face_ref[pair] * SIX, SIX) for pair in pairs]
        remotes = [
            eight_rows(incoming_ref[row, :]) - center_ref[block] for block, row in zip(blocks, rows)
        ]
        operands = [remote_operands(remote) for remote in remotes]
        products = [
            lax.dot_general(
                feature_ref[block, :, : right.shape[0]], right, NN, preferred_element_type=F32
            )
            for block, (right, _) in zip(blocks, operands)
        ]
        for block, row, remote, (_, right), product in zip(
            blocks, rows, remotes, operands, products
        ):
            grad, curv = pair_coefficients(product)
            remote, local = pair_sums(grad, curv, left_ref[block], right, remote)
            back_ref[row, :] += remote[:SIX]
            sums_ref[block] += local
        return carry

    count = jnp.where(lax.axis_index("body") > 0, local_ref.shape[0] // 4, 0)
    lax.fori_loop(0, count, some, 0)


def main_kernel(
    arrived_ref, sums_in_ref, rows_ref, feature_ref, left_ref, center_ref,
    return_ref, terms_ref,
    sums_ref, list_ref, table_ref, sem,
    *buffers,
):
    peers = arrived_ref.shape[0] // MSG
    slots = 2 * peers
    num_blocks = terms_ref.shape[0]
    marks = arrived_ref[pl.ds(RET, peers, stride=MSG), :]
    wide = jnp.sum(marks, axis=0, keepdims=True)[:, :slots] - 1.0
    valid = wide >= 0.0
    slot = lax.broadcasted_iota(jnp.int32, (1, slots), 1)
    one = lax.broadcasted_iota(jnp.int32, (slots, slots), 0)
    before = (one < lax.broadcasted_iota(jnp.int32, (slots, slots), 1)).astype(BF16)
    ones = jnp.broadcast_to(valid.astype(F32), (16, slots)).astype(BF16)
    place = lax.dot_general(ones, before, NN, preferred_element_type=F32)[0:1]
    hot = (one.astype(F32) == place) & valid
    row = lax.broadcasted_iota(jnp.int32, (16, slots), 0)
    second = slot >= peers
    peer = jnp.where(second, slot - peers, slot).astype(F32)
    codes = jnp.where(row == 0, jnp.broadcast_to(wide, (16, slots)), 0.0)
    codes = jnp.where(row == 1, jnp.broadcast_to(peer, (16, slots)), codes)
    codes = jnp.where(row == 2, jnp.broadcast_to(second.astype(F32), (16, slots)), codes)
    ordered = lax.dot_general(
        codes.astype(BF16), hot.astype(F32).astype(BF16), NT, preferred_element_type=F32
    )
    ordered = ordered[:8].astype(jnp.int32)
    total = jnp.sum(valid.astype(F32), axis=1, keepdims=True).astype(jnp.int32)
    row = row[:8]
    base = ordered[1:2]
    shift = ordered[2:3] * SIX
    table = jnp.where(row == 0, ordered[0:1], 0)
    table = jnp.where(row == 1, base * MSG + shift, table)
    table = jnp.where(row == 2, base * RET + shift, table)
    list_ref[:, :slots] = jnp.where(row == 3, total, table)
    copy = pltpu.make_async_copy(list_ref, table_ref, sem)
    copy.start()
    sums_ref[0:num_blocks] = sums_in_ref[...]
    sums_ref[num_blocks] = jnp.zeros((8, 2 * LANES), F32)
    copy.wait()
    count = table_ref[3, 0]

    def listed(group, k):
        return jnp.clip(group * GROUP + k, 0, count - 1)

    def distances(group, dist_ref, right_ref, remote_ref):
        for k in range(GROUP):
            pair = listed(group, k)
            block = table_ref[0, pair]
            rows = eight_rows(arrived_ref[pl.ds(table_ref[1, pair], SIX), :]) - center_ref[block]
            right, sums_right = remote_operands(rows)
            remote_ref[k] = rows
            right_ref[k] = sums_right
            dist_ref[k] = lax.dot_general(
                feature_ref[block, :, : right.shape[0]], right, NN, preferred_element_type=F32
            )

    def sums(group, dist_ref, right_ref, remote_ref):
        for k in range(GROUP):
            pair = group * GROUP + k
            known = listed(group, k)
            block = table_ref[0, known]
            target = jnp.where(pair < count, block, num_blocks)
            grad, curv = pair_coefficients(dist_ref[k])
            remote, local = pair_sums(grad, curv, left_ref[block], right_ref[k], remote_ref[k])
            return_ref[pl.ds(table_ref[2, known], SIX), :] = remote[:SIX]
            sums_ref[target] += local

    sets = [buffers[k::IN_TURN] for k in range(IN_TURN)]

    def some_groups(step, carry):
        group = IN_TURN * step
        for k in range(1, IN_TURN):
            distances(group + k, *sets[k])
            sums(group + k - 1, *sets[k - 1])
        distances(group + IN_TURN, *sets[0])
        sums(group + IN_TURN - 1, *sets[-1])
        return carry

    @pl.when(count > 0)
    def _():
        distances(0, *sets[0])
        lax.fori_loop(
            0, (count + IN_TURN * GROUP - 1) // (IN_TURN * GROUP), some_groups, 0
        )

    for block in range(num_blocks):
        terms_ref[block] = own_terms(rows_ref[block], sums_ref[block])


def gather_kernel(plan_ref, returned_ref, terms_ref, total_ref):
    num_blocks = terms_ref.shape[0]
    pairs = (plan_ref.shape[0] - 1 - FACES) // 2
    total_ref[0:num_blocks] = terms_ref[...]
    count = plan_ref[2 * pairs]

    def some(step, carry):
        for k in range(UNROLL):
            pair = step * UNROLL + k
            block = jnp.where(pair < count, plan_ref[pairs + pair], num_blocks)
            total_ref[block, 0:SIX, :] += returned_ref[pl.ds(plan_ref[pair], SIX), :]
        return carry

    lax.fori_loop(0, (count + UNROLL - 1) // UNROLL, some, 0)


def finish_kernel(plan_ref, total_ref, back_ref, grad_ref, hess_ref, sum_ref):
    sum_ref[...] = total_ref[...]
    for face in range(FACES):
        block = plan_ref[plan_ref.shape[0] - FACES + face]
        sum_ref[block, 0:SIX, :] += back_ref[face * SIX : face * SIX + SIX, :]
    for block in range(sum_ref.shape[0] - 1):
        span = slice(block * LANES, (block + 1) * LANES)
        grad_ref[:, span] = SCALE * sum_ref[block, 0:3, :]
        hess_ref[:, span] = SCALE * sum_ref[block, 3:6, :]


def smem():
    return pl.BlockSpec(memory_space=pltpu.SMEM)


def vmem():
    return pl.BlockSpec(memory_space=pltpu.VMEM)


def limit(mib):
    return pltpu.CompilerParams(vmem_limit_bytes=mib << 20)


def on_chip(*shape, dtype=F32):
    return pltpu.VMEM(shape, dtype)


def held(*values):
    return [pltpu.with_memory_space_constraint(value, pltpu.VMEM) for value in values]


def exchange(rows, peers):
    count = rows.shape[0] // peers
    return lax.all_to_all(
        rows.reshape(peers, count, 1, LANES), "blk", split_axis=0, concat_axis=0, tiled=True
    ).reshape(rows.shape)


def per_device(
    positions, direction, pair_local, pair_peer, pair_shift, pair_count,
    face_index, cross_local, cross_face,
):
    num_blocks = positions.shape[1] // LANES
    peers = lax.axis_size("blk")
    faces = face_index.shape[0]
    setup = (
        on_chip(num_blocks, 8, LANES),
        on_chip(num_blocks, 2 * LANES, LANES, dtype=BF16),
        on_chip(num_blocks, 32, LANES, dtype=BF16),
        on_chip(num_blocks, 8, LANES),
    )
    send, face_rows, plan = pl.pallas_call(
        pack_kernel,
        name="pack",
        out_shape=(
            on_chip(peers * MSG, LANES),
            on_chip(faces * SIX, LANES),
            pltpu.SMEM((2 * pair_local.shape[0] + 1 + faces,), jnp.int32),
        ),
        in_specs=[smem()] * 5 + [vmem()] * 2,
        out_specs=(vmem(), vmem(), smem()),
        scratch_shapes=[
            pltpu.SMEM((peers,), jnp.int32),
            pltpu.VMEM((num_blocks, 8, LANES), F32),
        ],
    )(pair_local, pair_peer, pair_shift, pair_count, face_index, positions, direction)
    arrived = exchange(send, peers)
    incoming = from_behind(face_rows, "body", 1)
    sums, back, *local = pl.pallas_call(
        cross_kernel,
        name="cross",
        compiler_params=limit(8),
        out_shape=(on_chip(num_blocks, 8, 2 * LANES), on_chip(faces * SIX, LANES)) + setup,
        in_specs=[smem()] * 2 + [vmem()] * 3,
        out_specs=(vmem(),) * 6,
    )(cross_local, cross_face, positions, direction, *held(incoming))
    face_back = from_behind(back, "body", -1)
    outgoing, terms = pl.pallas_call(
        main_kernel,
        name="pairs",
        compiler_params=limit(8),
        out_shape=(on_chip(peers * RET, LANES), on_chip(num_blocks, 8, LANES)),
        in_specs=[vmem()] * 6,
        out_specs=(vmem(), vmem()),
        scratch_shapes=[
            pltpu.VMEM((num_blocks + 1, 8, 2 * LANES), F32),
            pltpu.VMEM((8, LANES), jnp.int32),
            pltpu.SMEM((8, LANES), jnp.int32),
            pltpu.SemaphoreType.DMA,
        ]
        + [pltpu.VMEM((GROUP, 2 * LANES, LANES), F32)] * IN_TURN
        + [pltpu.VMEM((GROUP, 32, LANES), BF16)] * IN_TURN
        + [pltpu.VMEM((GROUP, 8, LANES), F32)] * IN_TURN,
    )(*held(arrived, sums, *local))
    returned = exchange(outgoing, peers)
    total = pl.pallas_call(
        gather_kernel,
        name="gather",
        compiler_params=limit(8),
        out_shape=on_chip(num_blocks + 1, 8, LANES),
        in_specs=[smem()] + [vmem()] * 2,
        out_specs=vmem(),
    )(plan, *held(returned, terms))
    return pl.pallas_call(
        finish_kernel,
        name="finish",
        out_shape=[jax.ShapeDtypeStruct((3, num_blocks * LANES), F32)] * 2,
        in_specs=[smem()] + [vmem()] * 2,
        out_specs=(vmem(), vmem()),
        scratch_shapes=[pltpu.VMEM((num_blocks + 1, 8, LANES), F32)],
    )(plan, *held(total, face_back))


def solution(mesh):
    split_all = P(("blk", "body"))
    wide = P(None, ("blk", "body"))

    return jax.shard_map(
        per_device,
        mesh=mesh,
        in_specs=(wide, wide) + (split_all,) * 7,
        out_specs=(wide, wide),
        check_vma=False,
    )
```
